256 devices in a mesh: tile: 32 (over z, x), wave: 8 (over y, core).
Axes of the slice: x: 4, y: 4, z: 8, core: 2. Of those that a mesh axis runs over, the one named last changes fastest.
Arguments:
- electric: float32 [16, 2048, 2048], P('wave', 'tile'), may hold values from -6 to 6
- magnet_x: float32 [16, 2048, 2048], P('wave', 'tile'), may hold values from -6 to 6
- magnet_y: float32 [16, 2048, 2048], P('wave', 'tile'), may hold values from -6 to 6
- permittivity_table: float32 [16, 4], P('wave'), may hold values from 1.5 to 6
- material: int32 [2048, 2048], P('tile'), may hold values from 0 to 3
- monitor_rows: int32 [16, 256], P('wave'), may hold values from 0 to 2047, as said below
- targets: int32 [16, 4], P('wave'), may hold values from 0 to 2047
Outputs:
- gradient: float32 [2048, 2048], P('tile', 'wave')
- efficiency: float32 [16, 4], P('wave')
The draws below stay inside these ranges and needn't reach their ends.
Inputs may be any that keep to these rules, and one draw needn't show every extreme that they name: `monitor_rows`: line l of each wavelength lies in rows 8 l to 8 l + 7.
All inputs are finite; a program needn't handle non-finite values.
Results may differ from the reference program's by a relative error of at most 0.0003.
Values sent between devices are 32-bit elements; how exact they have to be, the bound alone decides.
No kernel may reach another device: no remote copies, remote signals or barrier semaphores. Data moves between devices by JAX's collectives and lax.ppermute only.
A program may use at most 128 MiB of HBM per device.

```python
import math
import jax
import jax.numpy as jnp
from jax import lax

NY = 2048
STEPS = 12
MATS = 4
GROUP_PLANES = 4
GROUPS = 2
NX = 2048
WAVES = 16


def draw_monitor_rows(key, part):
    inner = jax.random.randint(jax.random.fold_in(key, 71), (WAVES, NY // 8), 0, 8, dtype=jnp.int32)
    rows = inner + 8 * jnp.arange(NY // 8, dtype=jnp.int32)[None, :]
    rows = rows.at[0, 0].set(0)
    rows = rows.at[WAVES - 1, NY // 8 - 1].set(NY - 1)
    return rows


def with_ends(drawn, rng, smallest, high):
    dims = drawn.shape
    place = [jax.random.randint(jax.random.fold_in(rng, axis), (), 0, dims[axis]) for axis in range(len(dims))]
    drawn = drawn.at[tuple(place)].set(smallest)
    longest = dims.index(max(dims))
    place[longest] = (place[longest] + 1) % dims[longest]
    return drawn.at[tuple(place)].set(high)


def level_of(key, dims, split, low, largest):
    loudness, own = 1.0, jax.random.fold_in(key, 6)
    for axis_at, shards_of in split:
        steps = jnp.exp(jax.random.uniform(jax.random.fold_in(own, axis_at), (shards_of,), jnp.float32, low / len(split), largest / len(split)))
        loudness = loudness * jnp.repeat(steps, dims[axis_at] // shards_of).reshape([-1 if axis == axis_at else 1 for axis in range(len(dims))])
    return loudness


def centred(stream_key, dims, width, bound, cuts=(), kind=jnp.bfloat16):
    array = width * jax.random.normal(stream_key, dims, jnp.float32)
    if cuts:
        array = array * level_of(stream_key, dims, cuts, -0.22, 0.18)
    return jnp.clip(array, -bound, bound).astype(kind)


def setup_inputs(seed: int = 0) -> dict:
    splits = jax.random.split(jax.random.key(seed), 8)
    return {
        "electric": centred(splits[0], (WAVES, NX, NY), 1.0, 6.0, ((0, 8), (1, 32)), jnp.float32),
        "magnet_x": centred(splits[1], (WAVES, NX, NY), 1.0, 6.0, ((0, 8), (1, 32)), jnp.float32),
        "magnet_y": centred(splits[2], (WAVES, NX, NY), 1.0, 6.0, ((0, 8), (1, 32)), jnp.float32),
        "permittivity_table": jnp.clip(1.5 + 4.5 * jax.random.uniform(splits[3], (WAVES, MATS), jnp.float32) ** level_of(splits[3], (WAVES, MATS), ((0, 8),), -0.2, 0.2), 1.5, 6.0),
        "material": with_ends(jax.random.randint(splits[4], (NX, NY), 0, MATS), jax.random.fold_in(splits[4], 1), 0, MATS - 1).astype(jnp.int32),
        "monitor_rows": draw_monitor_rows(jax.random.fold_in(splits[7], 71), 0),
        "targets": with_ends(jax.random.randint(splits[6], (WAVES, GROUP_PLANES), 0, NX), jax.random.fold_in(splits[6], 1), 0, NX - 1).astype(jnp.int32),
    }


half_step = 0.5
period = 8192
small_eps = 1e-06

def kernel_pair(wave_id, plane, offset, kernel_scale):
    chirp_rate = 1 + (37 * plane + 101 * wave_id) % 509
    phase_index = offset * offset % period * chirp_rate % period
    phase_angle = phase_index.astype(jnp.float32) * (2.0 * math.pi / period)
    return (jnp.cos(phase_angle) * kernel_scale, jnp.sin(phase_angle) * kernel_scale)

def yee_forward(efield, xfield, yfield, update_rate, monitor, angular):

    def advance(state_now, step_index):
        efield, xfield, yfield, spectrum_real, spectrum_imag = state_now
        zero_row = jnp.zeros_like(efield[:1])
        zero_column = jnp.zeros_like(efield[:, :1])
        shifted_x = jnp.concatenate([efield[1:], zero_row], 0)
        shifted_y = jnp.concatenate([efield[:, 1:], zero_column], 1)
        xfield_new = xfield - half_step * (shifted_y - efield)
        yfield_new = yfield + half_step * (shifted_x - efield)
        yfield_prev = jnp.concatenate([zero_row, yfield_new[:-1]], 0)
        xfield_prev = jnp.concatenate([zero_column, xfield_new[:, :-1]], 1)
        rotation = yfield_new - yfield_prev - (xfield_new - xfield_prev)
        efield_new = efield + update_rate * rotation
        monitor_line = lax.optimization_barrier(jnp.sum(jnp.take(efield_new, monitor, axis=1), axis=1))
        phase_now = angular * (step_index + 1).astype(jnp.float32)
        spectrum_real = spectrum_real + monitor_line * jnp.cos(phase_now)
        spectrum_imag = spectrum_imag - monitor_line * jnp.sin(phase_now)
        return ((efield_new, xfield_new, yfield_new, spectrum_real, spectrum_imag), None)
    start_state = (efield, xfield, yfield, jnp.zeros((NX,), jnp.float32), jnp.zeros((NX,), jnp.float32))
    final_state, _ = lax.scan(advance, start_state, jnp.arange(STEPS, dtype=jnp.int32))
    return (final_state[3], final_state[4])

def reference(electric, magnet_x, magnet_y, permittivity_table, material, monitor_rows, targets):
    focal_cells = jnp.arange(NX, dtype=jnp.int32)
    offset = focal_cells[:, None] - focal_cells[None, :]
    kernel_scale = 1.0 / math.sqrt(NX)

    def one_wave(running, inputs):
        wave_id, efield, xfield, yfield, table_row, monitor, target_row = inputs
        permittivity = table_row[material]
        update_rate = half_step / permittivity
        angular = 0.3 + 0.05 * wave_id.astype(jnp.float32)

        def evolve(rate_field):
            return yee_forward(efield, xfield, yfield, rate_field, monitor, angular)
        spectrum_real, spectrum_imag = evolve(update_rate)
        back_real = jnp.zeros((NX,), jnp.float32)
        back_imag = jnp.zeros((NX,), jnp.float32)
        gains = []
        for plane_pos in range(GROUP_PLANES):
            plane = GROUP_PLANES * (wave_id % GROUPS) + plane_pos
            kern_cos, kern_sin = kernel_pair(wave_id, plane, offset, kernel_scale)
            focal_real = lax.optimization_barrier(jnp.sum(kern_cos * spectrum_real[None, :] - kern_sin * spectrum_imag[None, :], axis=1))
            focal_imag = lax.optimization_barrier(jnp.sum(kern_sin * spectrum_real[None, :] + kern_cos * spectrum_imag[None, :], axis=1))
            intensity = focal_real * focal_real + focal_imag * focal_imag
            on_target = (focal_cells == target_row[plane_pos]).astype(jnp.float32)
            target_power = jnp.sum(intensity * on_target)
            total_power = jnp.sum(intensity)
            mean_power = total_power / NX + small_eps
            gains.append(target_power / mean_power)
            weight = on_target / mean_power - target_power / (mean_power * mean_power * NX)
            focal_bar_real = 2.0 * focal_real * weight
            focal_bar_imag = 2.0 * focal_imag * weight
            back_real = back_real + lax.optimization_barrier(jnp.sum(kern_cos * focal_bar_real[:, None] + kern_sin * focal_bar_imag[:, None], axis=0))
            back_imag = back_imag + lax.optimization_barrier(jnp.sum(-kern_sin * focal_bar_real[:, None] + kern_cos * focal_bar_imag[:, None], axis=0))
        _, pull_back = jax.vjp(evolve, update_rate)
        rate_bar, = pull_back((back_real, back_imag))
        wave_gradient = rate_bar * (-half_step / (permittivity * permittivity))
        return (running + wave_gradient, jnp.stack(gains))
    inputs = (jnp.arange(WAVES, dtype=jnp.int32), electric, magnet_x, magnet_y, permittivity_table, monitor_rows, targets)
    gradient, efficiency = lax.scan(one_wave, jnp.zeros((NX, NY), jnp.float32), inputs)
    return (gradient, efficiency)
```

```python
import functools
import math

import jax
import jax.numpy as jnp
from jax import lax
from jax.experimental import pallas as pl
from jax.experimental.pallas import tpu as pltpu
from jax.sharding import PartitionSpec as P

STEPS = 12
GROUP_PLANES = 4
GROUPS = 2
PERIOD = 8192
SMALL = 1e-06

LANES = 128
ROWS = 64
HALO = 12
BASE = 24
EXT = 112
OWN_LO = BASE // 8
OWN_HI = (BASE + ROWS) // 8
NFREE = 64

VMEM = pltpu.VMEM
VSPEC = pl.BlockSpec(memory_space=pltpu.VMEM)
SSPEC = pl.BlockSpec(memory_space=pltpu.SMEM)
ASPEC = pl.BlockSpec(memory_space=pl.ANY)
HIGHEST = lax.Precision.HIGHEST


def cos_of(phase):
    phase = phase & (PERIOD - 1)
    quadrant = (phase + 1024) >> 11
    angle = (phase - (quadrant << 11)).astype(jnp.float32) * (2.0 * math.pi / PERIOD)
    sq = angle * angle
    even = 1.0 + sq * (-1 / 2 + sq * (1 / 24 + sq * (-1 / 720 + sq * (1 / 40320))))
    odd = angle * (1.0 + sq * (-1 / 6 + sq * (1 / 120 + sq * (-1 / 5040 + sq * (1 / 362880)))))
    value = jnp.where((quadrant & 1) == 1, odd, even)
    return jnp.where(((quadrant + 1) & 2) != 0, -value, value)


def iota2(shape, axis):
    return lax.broadcasted_iota(jnp.int32, shape, axis)


def table_kernel(tiles, scale, rate_ref, left_ref, right_ref, back_ref, last_ref, twist_ref, chirp_ref):
    quarter = PERIOD // 4
    unit = PERIOD // NFREE

    def one(combo, carry):
        rate = rate_ref[combo]
        shape = (2 * NFREE, 2 * tiles)
        row, col = iota2(shape, 0), iota2(shape, 1)
        part = jnp.where(col >= tiles, 1, 0) - jnp.where(row >= NFREE, 1, 0)
        phase = ((row & (NFREE - 1)) * (col & (tiles - 1)) * rate & (NFREE - 1)) * unit
        left_ref[combo] = cos_of(part * quarter - phase)
        shape = (NFREE, tiles)
        phase = (iota2(shape, 0) * iota2(shape, 1) * rate & (NFREE - 1)) * unit
        right_ref[combo, 0] = cos_of(phase)
        right_ref[combo, 1] = cos_of(phase + quarter)
        shape = (tiles, NFREE)
        phase = (iota2(shape, 0) * iota2(shape, 1) * rate & (NFREE - 1)) * unit
        back_ref[combo, 0] = cos_of(phase)
        back_ref[combo, 1] = cos_of(phase - quarter)
        shape = (2 * tiles, 2 * NFREE)
        row, col = iota2(shape, 0), iota2(shape, 1)
        part = jnp.where(col >= NFREE, 1, 0) - jnp.where(row >= tiles, 1, 0)
        phase = ((row & (tiles - 1)) * (col & (NFREE - 1)) * rate & (NFREE - 1)) * unit
        last_ref[combo] = cos_of(part * quarter + phase)
        shape = (NFREE, NFREE)
        phase = (iota2(shape, 0) * iota2(shape, 1) * rate & (PERIOD // 2 - 1)) * 2
        twist_ref[combo, 0] = cos_of(phase)
        twist_ref[combo, 1] = cos_of(phase + quarter)
        shape = (tiles, NFREE)
        cell = iota2(shape, 0) * NFREE + iota2(shape, 1)
        phase = (cell * cell & (PERIOD - 1)) * rate
        chirp_ref[combo, 0] = cos_of(phase) * scale
        chirp_ref[combo, 1] = cos_of(phase - quarter) * scale
        return carry

    lax.fori_loop(0, rate_ref.shape[0], one, 0)


def group_rows(group):
    return pl.multiple_of(group * 8, 8)


def bounds(step, first, last):
    low = jnp.where(step < 3, 1, jnp.where(step < STEPS - 1, 2, OWN_LO))
    high = jnp.where(step < 3, OWN_HI + 2, jnp.where(step < STEPS - 1, OWN_HI + 1, OWN_HI))
    return jnp.where(first, OWN_LO, low), jnp.where(last, OWN_HI, high)


def forward_kernel(
    wave, tiles, cols,
    tile_ref, coef_ref, rate_ref, e_hbm, x_hbm, y_hbm, mat_hbm, left_ref, right_ref, mleft_ref, mright_ref, hot_ref,
    rot_ref, spec_ref, q_ref,
    e_ref, x_ref, y_ref, mat_ref, line_ref, sems,
):
    tile = tile_ref[0]
    first, last = tile == 0, tile == tiles - 1
    copies = []
    for field, (src, dst) in enumerate(((e_hbm, e_ref), (x_hbm, x_ref), (y_hbm, y_ref))):
        for j in range(cols):
            copies.append(pltpu.make_async_copy(
                src.at[wave, :, pl.ds(j * LANES, LANES)], dst.at[j, pl.ds(BASE, ROWS), :], sems.at[field, j]))
    for j in range(cols):
        copies.append(pltpu.make_async_copy(
            mat_hbm.at[:, pl.ds(j * LANES, LANES)], mat_ref.at[j], sems.at[3, j]))
    for copy in copies:
        copy.start()

    def rate_of(mat):
        value = jnp.full(mat.shape, rate_ref[wave, 0], jnp.float32)
        for kind in range(1, rate_ref.shape[1]):
            value = jnp.where(mat == kind, rate_ref[wave, kind], value)
        return value

    hi = BASE + ROWS
    for j in range(cols):
        lanes = pl.ds(j * LANES, LANES)
        for src, msrc, start in ((left_ref, mleft_ref, BASE - HALO), (right_ref, mright_ref, hi)):
            rows = pl.ds(start, HALO)
            e_ref[j, rows, :] = src[0:HALO, lanes] * 0.5
            x_ref[j, rows, :] = src[HALO:2 * HALO, lanes]
            y_ref[j, rows, :] = src[2 * HALO:3 * HALO, lanes]
            q_ref[j, rows, :] = rate_of(msrc[3 * HALO:4 * HALO, lanes].astype(jnp.int32))
    line_ref[...] = jnp.zeros(line_ref.shape, jnp.float32)
    for copy in copies:
        copy.wait()

    def prepare(group, carry):
        own = pl.ds(group_rows(group - OWN_LO), 8)
        rows = pl.ds(group_rows(group), 8)
        for j in range(cols):
            e_ref[j, rows, :] = e_ref[j, rows, :] * 0.5
            q_ref[j, rows, :] = rate_of(mat_ref[j, own, :])
        return carry

    lax.fori_loop(OWN_LO, OWN_HI, prepare, 0)
    lane = lax.broadcasted_iota(jnp.int32, (8, LANES), 1)
    end_lane, start_lane = lane == LANES - 1, lane == 0

    def step(index, carry):
        low, high = bounds(index, first, last)
        low_y = jnp.where(first, OWN_LO, jnp.where(index < 4, 1, 2))

        def turn_y(group, inner):
            base = group_rows(group)
            for j in range(cols):
                now = e_ref[j, pl.ds(base, 8), :]
                y_ref[j, pl.ds(base, 8), :] = y_ref[j, pl.ds(base, 8), :] + (e_ref[j, pl.ds(base + 1, 8), :] - now)
            return inner

        lax.fori_loop(low_y, high, turn_y, 0)

        def turn_e(own, group, inner):
            base = group_rows(group)
            rows = pl.ds(base, 8)
            own_rows = pl.ds(group_rows(group - OWN_LO), 8)
            efield = [e_ref[j, rows, :] for j in range(cols)]
            rolled = [pltpu.roll(value, LANES - 1, 1) for value in efield]
            rolled.append(jnp.zeros((8, LANES), jnp.float32))
            before = jnp.zeros((8, LANES), jnp.float32)
            total = None
            for j in range(cols):
                shifted = jnp.where(end_lane, rolled[j + 1], rolled[j])
                xfield = x_ref[j, rows, :] - (shifted - efield[j])
                x_ref[j, rows, :] = xfield
                turned = pltpu.roll(xfield, 1, 1)
                xprev = jnp.where(start_lane, before, turned)
                before = turned
                rotation = (y_ref[j, rows, :] - y_ref[j, pl.ds(base - 1, 8), :]) - (xfield - xprev)
                enew = efield[j] + q_ref[j, rows, :] * rotation
                e_ref[j, rows, :] = enew
                if own:
                    rot_ref[index, j, own_rows, :] = rotation
                    term = enew * hot_ref[wave, j:j + 1, :]
                    total = term if total is None else total + term
            if own:
                line_ref[0, own_rows, :] = line_ref[0, own_rows, :] + total * coef_ref[wave, 0, index]
                line_ref[1, own_rows, :] = line_ref[1, own_rows, :] + total * coef_ref[wave, 1, index]
            return inner

        lax.fori_loop(low, OWN_LO, functools.partial(turn_e, False), 0)
        lax.fori_loop(OWN_LO, OWN_HI, functools.partial(turn_e, True), 0)
        lax.fori_loop(OWN_HI, high, functools.partial(turn_e, False), 0)
        return carry

    lax.fori_loop(0, STEPS, step, 0)
    both = line_ref[...].reshape(2 * ROWS, LANES)
    spec_ref[...] = lax.dot_general(
        jnp.ones((8, LANES), jnp.float32), both, (((1,), (1,)), ((), ())),
        precision=HIGHEST, preferred_element_type=jnp.float32)


def dot(left, right):
    return jnp.dot(left, right, precision=HIGHEST, preferred_element_type=jnp.float32)


def turned(stacked):
    half = stacked.shape[0] // 2
    return jnp.concatenate([-stacked[half:], stacked[:half]], 0)


def chirp_part(tiles, waves, tile, tgt_ref, spectra_ref, tabs, eff_ref, bar_ref):
    left_ref, right_ref, back_ref, last_ref, twist_ref, chirp_ref = tabs
    count = tiles * NFREE
    pixel = iota2((NFREE, tiles), 1) * NFREE + iota2((NFREE, tiles), 0)
    srow, slane = iota2((8, LANES), 0), iota2((8, LANES), 1)
    effs = jnp.zeros((8, LANES), jnp.float32)
    spots = iota2((tiles, LANES), 0)
    for wave in range(waves):
        real = spectra_ref[:, wave * LANES:wave * LANES + NFREE]
        imag = spectra_ref[:, wave * LANES + NFREE:(wave + 1) * LANES]
        bar_real = jnp.zeros((tiles, NFREE), jnp.float32)
        bar_imag = jnp.zeros((tiles, NFREE), jnp.float32)
        for plane in range(GROUP_PLANES):
            combo = wave * GROUP_PLANES + plane
            ch_r, ch_i = chirp_ref[combo, 0], chirp_ref[combo, 1]
            tw_r, tw_i = twist_ref[combo, 0], twist_ref[combo, 1]
            source = jnp.concatenate([ch_r * real - ch_i * imag, ch_r * imag + ch_i * real], 0)
            stage = dot(left_ref[combo], source)
            st_r, st_i = stage[:NFREE], stage[NFREE:]
            mid = jnp.concatenate([tw_r * st_r - tw_i * st_i, tw_r * st_i + tw_i * st_r], 0)
            focal = dot(mid, right_ref[combo, 0]) + dot(turned(mid), right_ref[combo, 1])
            f_r, f_i = focal[:NFREE], focal[NFREE:]
            intensity = f_r * f_r + f_i * f_i
            on_target = (pixel == tgt_ref[wave, plane]).astype(jnp.float32)
            target_power = jnp.sum(jnp.sum(intensity * on_target, 0, keepdims=True), 1, keepdims=True)
            total_power = jnp.sum(jnp.sum(intensity, 0, keepdims=True), 1, keepdims=True)
            mean_power = total_power / count + SMALL
            efficiency = target_power / mean_power
            weight = on_target / mean_power - target_power / (mean_power * mean_power * count)
            effs = jnp.where((srow == wave) & (slane == plane), efficiency, effs)
            double = 2.0 * weight
            bar = jnp.concatenate([f_r * double, f_i * double], 0)
            stage = dot(bar, back_ref[combo, 0]) + dot(turned(bar), back_ref[combo, 1])
            st_r, st_i = stage[:NFREE], stage[NFREE:]
            mid = jnp.concatenate([tw_r * st_r + tw_i * st_i, tw_r * st_i - tw_i * st_r], 0)
            line = dot(last_ref[combo], mid)
            l_r, l_i = line[:tiles], line[tiles:]
            bar_real = bar_real + ch_r * l_r + ch_i * l_i
            bar_imag = bar_imag + ch_r * l_i - ch_i * l_r
        for part, value in enumerate((bar_real, bar_imag)):
            for where, lo, hi, at in ((-1, NFREE - 16, NFREE, BASE - 16), (0, 0, NFREE, BASE), (1, 0, 16, BASE + ROWS)):
                chosen = (spots == tile + where).astype(jnp.float32)
                spread = lax.dot_general(
                    value, chosen, (((0,), (0,)), ((), ())), precision=HIGHEST, preferred_element_type=jnp.float32)
                bar_ref[wave, part, at:at + hi - lo, :] = spread[lo:hi]
    eff_ref[...] = effs


def adjoint_kernel(
    waves, tiles, cols,
    tile_ref, coef_ref, tgt_ref, spectra_ref, left_ref, right_ref, back_ref, last_ref, twist_ref, chirp_ref,
    hot_ref, rot0_ref, rot1_ref, q0_ref, q1_ref,
    grad_ref, eff_ref,
    bar_ref, e_ref, x_ref, y_ref, s_ref, prod_ref,
):
    tile = tile_ref[0]
    first, last = tile == 0, tile == tiles - 1
    chirp_part(
        tiles, waves, tile, tgt_ref, spectra_ref,
        (left_ref, right_ref, back_ref, last_ref, twist_ref, chirp_ref), eff_ref, bar_ref)
    lane = lax.broadcasted_iota(jnp.int32, (8, LANES), 1)
    end_lane, start_lane = lane == LANES - 1, lane == 0
    zero = jnp.zeros((8, LANES), jnp.float32)
    for wave, (rot_ref, q_ref) in enumerate(((rot0_ref, q0_ref), (rot1_ref, q1_ref))):

        def clear(group, carry):
            rows = pl.ds(group_rows(group), 8)
            for j in range(cols):
                e_ref[j, rows, :] = zero
                x_ref[j, rows, :] = zero
                y_ref[j, rows, :] = zero
                s_ref[j, rows, :] = zero
            return carry

        lax.fori_loop(0, EXT // 8, clear, 0)

        def clear_own(group, carry):
            rows = pl.ds(group_rows(group), 8)
            for j in range(cols):
                prod_ref[j, rows, :] = zero
            return carry

        lax.fori_loop(0, ROWS // 8, clear_own, 0)

        def pushed(base, index):
            rows = pl.ds(base, 8)
            return (bar_ref[wave, 0, rows, :] * coef_ref[wave, 0, index]
                    + bar_ref[wave, 1, rows, :] * coef_ref[wave, 1, index])

        def lit(base, j, push):
            rows = pl.ds(base, 8)
            return (e_ref[j, rows, :] + (y_ref[j, pl.ds(base - 1, 8), :] - y_ref[j, rows, :])
                    + push * hot_ref[wave, j:j + 1, :])

        def step(count, carry):
            index = STEPS - 1 - count
            low, high = bounds(count, first, last)

            def turn_e(own, group, inner):
                base = group_rows(group)
                rows = pl.ds(base, 8)
                own_rows = pl.ds(group_rows(group - OWN_LO), 8)
                push = pushed(base, index)
                efield, scaled = [], []
                for j in range(cols):
                    value = lit(base, j, push)
                    efield.append(value)
                    if own:
                        prod_ref[j, own_rows, :] = prod_ref[j, own_rows, :] + value * rot_ref[index, j, own_rows, :]
                    value = q_ref[j, rows, :] * value
                    s_ref[j, rows, :] = value
                    scaled.append(value)
                rolled = [pltpu.roll(value, LANES - 1, 1) for value in scaled]
                rolled.append(zero)
                before = zero
                for j in range(cols):
                    shifted = jnp.where(end_lane, rolled[j + 1], rolled[j])
                    xfield = x_ref[j, rows, :] + (shifted - scaled[j])
                    x_ref[j, rows, :] = xfield
                    turn = pltpu.roll(xfield, 1, 1)
                    xprev = jnp.where(start_lane, before, turn)
                    before = turn
                    e_ref[j, rows, :] = efield[j] + (xfield - xprev)
                return inner

            lax.fori_loop(low, OWN_LO, functools.partial(turn_e, False), 0)
            lax.fori_loop(OWN_LO, OWN_HI, functools.partial(turn_e, True), 0)
            lax.fori_loop(OWN_HI, high, functools.partial(turn_e, False), 0)

            def turn_y(group, inner):
                base = group_rows(group)
                rows = pl.ds(base, 8)
                for j in range(cols):
                    y_ref[j, rows, :] = y_ref[j, rows, :] + (s_ref[j, rows, :] - s_ref[j, pl.ds(base + 1, 8), :])
                return inner

            lax.fori_loop(low, high, turn_y, 0)
            return carry

        lax.fori_loop(0, STEPS - 1, step, 0)

        def finish(group, carry):
            base = group_rows(group)
            rows = pl.ds(base, 8)
            own_rows = pl.ds(group_rows(group - OWN_LO), 8)
            push = pushed(base, 0)
            for j in range(cols):
                total = prod_ref[j, own_rows, :] + lit(base, j, push) * rot_ref[0, j, own_rows, :]
                rate = q_ref[j, rows, :]
                value = total * (-8.0 * (rate * rate))
                place = pl.ds((j % 2) * LANES, LANES)
                if wave:
                    value = value + grad_ref[j // 2, own_rows, place]
                grad_ref[j // 2, own_rows, place] = value
            return carry

        lax.fori_loop(OWN_LO, OWN_HI, finish, 0)


def per_device(electric, magnet_x, magnet_y, permittivity_table, material, monitor_rows, targets):
    waves, rows, depth = electric.shape
    tiles = lax.axis_size("tile")
    parts = lax.axis_size("wave")
    cols = depth // LANES
    f32 = jnp.float32
    tile_pos = lax.axis_index("tile")
    tile_arr = tile_pos.astype(jnp.int32)[None]
    wave_ids = lax.axis_index("wave") * waves + jnp.arange(waves, dtype=jnp.int32)
    mat_f = material.astype(f32)
    params = pltpu.CompilerParams(vmem_limit_bytes=56 * 1024 * 1024)

    up = [(s, s + 1) for s in range(tiles - 1)]
    down = [(s + 1, s) for s in range(tiles - 1)]
    halos = []
    for wave in range(waves):
        tops = [v[wave, :HALO] for v in (electric, magnet_x, magnet_y)]
        ends = [v[wave, rows - HALO:] for v in (electric, magnet_x, magnet_y)]
        if wave == 0:
            tops.append(mat_f[:HALO])
            ends.append(mat_f[rows - HALO:])
        halos.append((
            lax.ppermute(jnp.concatenate(ends, 0), "tile", up),
            lax.ppermute(jnp.concatenate(tops, 0), "tile", down),
        ))

    planes = GROUP_PLANES * (wave_ids % GROUPS)[:, None] + jnp.arange(GROUP_PLANES, dtype=jnp.int32)[None, :]
    chirp_rates = (1 + (37 * planes + 101 * wave_ids[:, None]) % 509).reshape(-1)
    combos = waves * GROUP_PLANES
    tables = pl.pallas_call(
        functools.partial(table_kernel, tiles, 1.0 / math.sqrt(rows * tiles)),
        out_shape=(
            jax.ShapeDtypeStruct((combos, 2 * NFREE, 2 * tiles), f32),
            jax.ShapeDtypeStruct((combos, 2, NFREE, tiles), f32),
            jax.ShapeDtypeStruct((combos, 2, tiles, NFREE), f32),
            jax.ShapeDtypeStruct((combos, 2 * tiles, 2 * NFREE), f32),
            jax.ShapeDtypeStruct((combos, 2, NFREE, NFREE), f32),
            jax.ShapeDtypeStruct((combos, 2, tiles, NFREE), f32),
        ),
        in_specs=[SSPEC],
        out_specs=(VSPEC,) * 6,
        compiler_params=params,
        name="tables",
    )(chirp_rates)

    row_ids = jnp.arange(depth, dtype=jnp.int32)
    block = depth // monitor_rows.shape[1]
    hot = (jnp.repeat(monitor_rows, block, axis=1) == row_ids[None, :]).astype(f32).reshape(waves, cols, LANES)
    angular = 0.3 + 0.05 * wave_ids.astype(f32)
    phase = angular[:, None] * jnp.arange(1, STEPS + 1, dtype=jnp.int32).astype(f32)[None, :]
    coef = jnp.stack([jnp.cos(phase), -jnp.sin(phase)], 1)
    rates = 0.25 / permittivity_table

    ext = (cols, EXT, LANES)
    spectra, rotations, qs = [], [], []
    for wave in range(waves):
        rot, spec, q = pl.pallas_call(
            functools.partial(forward_kernel, wave, tiles, cols),
            out_shape=(
                jax.ShapeDtypeStruct((STEPS, cols, rows, LANES), f32),
                jax.ShapeDtypeStruct((8, LANES), f32),
                jax.ShapeDtypeStruct(ext, f32),
            ),
            in_specs=[SSPEC, SSPEC, SSPEC, ASPEC, ASPEC, ASPEC, ASPEC, VSPEC, VSPEC, VSPEC, VSPEC, VSPEC],
            out_specs=(VSPEC, VSPEC, VSPEC),
            scratch_shapes=[
                VMEM(ext, f32), VMEM(ext, f32), VMEM(ext, f32),
                VMEM((cols, rows, LANES), jnp.int32), VMEM((2, rows, LANES), f32),
                pltpu.SemaphoreType.DMA((4, cols)),
            ],
            compiler_params=params,
            name="forward",
        )(tile_arr, 2.0 * coef, rates, electric, magnet_x, magnet_y, material,
          halos[wave][0], halos[wave][1], halos[0][0], halos[0][1], hot)
        rotations.append(rot)
        spectra.append(spec[:1])
        qs.append(q)

    line = jnp.broadcast_to(jnp.concatenate(spectra, 1), (tiles, waves * LANES))
    gathered = lax.all_to_all(line, "tile", 0, 0, tiled=True)

    grad, eff = pl.pallas_call(
        functools.partial(adjoint_kernel, waves, tiles, cols),
        out_shape=(
            jax.ShapeDtypeStruct((parts, rows, depth // parts), f32),
            jax.ShapeDtypeStruct((8, LANES), f32),
        ),
        in_specs=[SSPEC, SSPEC, SSPEC] + [VSPEC] * 12,
        out_specs=(VSPEC, VSPEC),
        scratch_shapes=[
            VMEM((waves, 2, EXT, LANES), f32),
            VMEM(ext, f32), VMEM(ext, f32), VMEM(ext, f32), VMEM(ext, f32),
            VMEM((cols, rows, LANES), f32),
        ],
        compiler_params=params,
        name="adjoint",
    )(tile_arr, coef, targets, gathered, *tables, hot, *rotations, *qs)
    efficiency = eff[:waves, :GROUP_PLANES]

    mine = lax.axis_index("wave")
    core, chip = mine % 2, mine // 2
    pairs = grad.reshape(parts // 2, 2, rows, depth // parts)
    kept = lax.dynamic_index_in_dim(pairs, core, 1, keepdims=False)
    given = lax.dynamic_index_in_dim(pairs, 1 - core, 1, keepdims=False)
    half = kept + lax.ppermute(given, "wave", [(s, s ^ 1) for s in range(parts)])
    chips = parts // 2
    gradient = lax.dynamic_index_in_dim(half, chip, 0, keepdims=False)
    for hop in range(1, chips):
        piece = lax.dynamic_index_in_dim(half, (chip + hop) % chips, 0, keepdims=False)
        gradient = gradient + lax.ppermute(
            piece, "wave", [(s, (s // 2 + hop) % chips * 2 + s % 2) for s in range(parts)])
    return gradient, efficiency


def solution(mesh):
    in_specs = (
        P("wave", "tile", None),
        P("wave", "tile", None),
        P("wave", "tile", None),
        P("wave", None),
        P("tile", None),
        P("wave", None),
        P("wave", None),
    )
    out_specs = (P("tile", "wave"), P("wave", None))
    return jax.shard_map(
        per_device, mesh=mesh, in_specs=in_specs, out_specs=out_specs, check_vma=False
    )
```

```python
import functools
import math

import jax
import jax.numpy as jnp
from jax import lax
from jax.experimental import pallas as pl
from jax.experimental.pallas import tpu as pltpu
from jax.sharding import PartitionSpec as P

STEPS = 12
GROUP_PLANES = 4
GROUPS = 2
PERIOD = 8192
SMALL = 1e-06

LANES = 128
ROWS = 64
HALO = 12
BASE = 24
EXT = 112
OWN_LO = BASE // 8
OWN_HI = (BASE + ROWS) // 8
NFREE = 64

VMEM_LEAN = 40
VMEM_FULL = 56
VMEM = pltpu.VMEM
VSPEC = pl.BlockSpec(memory_space=pltpu.VMEM)
SSPEC = pl.BlockSpec(memory_space=pltpu.SMEM)
ASPEC = pl.BlockSpec(memory_space=pl.ANY)
HSPEC = pl.BlockSpec(memory_space=pltpu.HBM)
HIGHEST = lax.Precision.HIGHEST


def cos_sin(phase):
    phase = phase & (PERIOD - 1)
    quadrant = (phase + 1024) >> 11
    angle = (phase - (quadrant << 11)).astype(jnp.float32) * (2.0 * math.pi / PERIOD)
    sq = angle * angle
    even = 1.0 + sq * (-1 / 2 + sq * (1 / 24 + sq * (-1 / 720 + sq * (1 / 40320))))
    odd = angle * (1.0 + sq * (-1 / 6 + sq * (1 / 120 + sq * (-1 / 5040 + sq * (1 / 362880)))))
    swap = (quadrant & 1) == 1
    cosine = jnp.where(swap, odd, even)
    sine = jnp.where(swap, even, odd)
    cosine = jnp.where(((quadrant + 1) & 2) != 0, -cosine, cosine)
    return cosine, jnp.where((quadrant & 2) != 0, -sine, sine)


def halves(value):
    high = value.astype(jnp.bfloat16)
    return high, (value - high.astype(jnp.float32)).astype(jnp.bfloat16)


def iota2(shape, axis):
    return lax.broadcasted_iota(jnp.int32, shape, axis)


def table_kernel(tiles, waves, scale, left_ref, right_ref, back_ref, last_ref, twist_ref, chirp_ref):
    unit = PERIOD // NFREE
    mine = lax.axis_index("wave")

    def one(combo, carry):
        wave = mine * waves + lax.div(combo, GROUP_PLANES)
        plane = GROUP_PLANES * lax.rem(wave, GROUPS) + lax.rem(combo, GROUP_PLANES)
        rate = 1 + lax.rem(37 * plane + 101 * wave, 509)

        def put(ref, slot, value):
            for which, part in enumerate(halves(value)):
                if slot is None:
                    ref[combo, which] = part
                else:
                    ref[combo, slot, which] = part

        shape = (NFREE, tiles)
        cosine, sine = cos_sin((iota2(shape, 0) * iota2(shape, 1) * rate & (NFREE - 1)) * unit)
        put(right_ref, 0, cosine)
        put(right_ref, 1, -sine)
        put(left_ref, None, jnp.concatenate(
            [jnp.concatenate([cosine, sine], 1), jnp.concatenate([-sine, cosine], 1)], 0))
        shape = (tiles, NFREE)
        cosine, sine = cos_sin((iota2(shape, 0) * iota2(shape, 1) * rate & (NFREE - 1)) * unit)
        put(back_ref, 0, cosine)
        put(back_ref, 1, sine)
        put(last_ref, None, jnp.concatenate(
            [jnp.concatenate([cosine, -sine], 1), jnp.concatenate([sine, cosine], 1)], 0))
        shape = (NFREE, NFREE)
        cosine, sine = cos_sin((iota2(shape, 0) * iota2(shape, 1) * rate & (PERIOD // 2 - 1)) * 2)
        twist_ref[combo, 0] = cosine
        twist_ref[combo, 1] = -sine
        shape = (tiles, NFREE)
        cell = iota2(shape, 0) * NFREE + iota2(shape, 1)
        cosine, sine = cos_sin((cell * cell & (PERIOD - 1)) * rate)
        chirp_ref[combo, 0] = cosine * scale
        chirp_ref[combo, 1] = sine * scale
        return carry

    lax.fori_loop(0, waves * GROUP_PLANES, one, 0)


def group_rows(group):
    return pl.multiple_of(group * 8, 8)


def bounds(step, first, last):
    low = jnp.where(step < 3, 1, jnp.where(step < STEPS - 1, 2, OWN_LO))
    high = jnp.where(step < 3, OWN_HI + 2, jnp.where(step < STEPS - 1, OWN_HI + 1, OWN_HI))
    return jnp.where(first, OWN_LO, low), jnp.where(last, OWN_HI, high)


def spread_columns(block_of, rows, flip_ref, cols, put):
    for j in range(cols):
        flip_ref[j * LANES:(j + 1) * LANES, :rows] = block_of(j).T
    for j in range(cols):
        put(j, flip_ref[pl.ds(j, LANES, stride=cols), :rows].T)


def edges_kernel(waves, e_hbm, x_hbm, y_hbm, mat_hbm, *refs):
    outs, (in_ref, mat_ref, sems) = refs[:2], refs[2:]
    span = 16
    copies = []
    for side, start in enumerate((ROWS - span, 0)):
        copies.append([pltpu.make_async_copy(mat_hbm.at[pl.ds(start, span), :], mat_ref.at[side], sems.at[side, 0, 3])])
        for wave in range(waves):
            copies.append([
                pltpu.make_async_copy(
                    src.at[wave, pl.ds(start, span), :], in_ref.at[side, wave, field], sems.at[side, wave, field])
                for field, src in enumerate((e_hbm, x_hbm, y_hbm))])
    for group in copies:
        for copy in group:
            copy.start()
    shape = in_ref.shape[3:]
    row, col = iota2(shape, 0), iota2(shape, 1)
    for side in range(2):
        for copy in copies[side * (waves + 1)]:
            copy.wait()
        for wave in range(waves):
            for copy in copies[side * (waves + 1) + 1 + wave]:
                copy.wait()
            out = outs[side].at[pl.ds(2 * HALO * wave, 2 * HALO), :]
            efield, xfield, yfield = in_ref[side, wave, 0], in_ref[side, wave, 1], in_ref[side, wave, 2]
            yprev = jnp.where(row == 0, 0.0, pltpu.roll(yfield, 1, 0))
            xprev = jnp.where(col == 0, 0.0, pltpu.roll(xfield, 1, 1))
            curl = (yfield - yprev) - (xfield - xprev)
            low = span - HALO
            if side:
                out[0:HALO, :] = efield[:HALO] * 0.5
                out[HALO:2 * HALO, :] = curl[:HALO]
            else:
                out[0:HALO, :] = efield[low:] * 0.5
                out[HALO:2 * HALO - 1, :] = curl[low + 1:]
                out[2 * HALO - 1:2 * HALO, :] = yfield[span - 1:]
        mat = mat_ref[side].astype(jnp.float32)
        outs[side][2 * HALO * waves:, :] = mat[:HALO] if side else mat[low:]


def prepare_kernel(
    waves, cols, e_hbm, x_hbm, y_hbm, mat_hbm, out_hbm, yend_ref,
    flip_ref, flip2_ref, xs_ref, ys_ref, e_ref, x_ref, y_ref, mat_ref, eout_ref, rout_ref, mout_ref, sems,
):
    both = waves * ROWS
    loads = [
        pltpu.make_async_copy(src, dst, sems.at[at])
        for at, (src, dst) in enumerate(((e_hbm, e_ref), (x_hbm, x_ref), (y_hbm, y_ref), (mat_hbm, mat_ref)))]
    stores = [
        pltpu.make_async_copy(src, dst, sems.at[4 + at])
        for at, (src, dst) in enumerate((
            (eout_ref, out_hbm.at[pl.ds(0, waves)]), (rout_ref, out_hbm.at[pl.ds(waves, waves)]),
            (mout_ref, out_hbm.at[2 * waves])))]
    for copy in loads:
        copy.start()

    def block(ref):
        return lambda j: ref[:, :, j * LANES:(j + 1) * LANES].reshape(both, LANES)

    def put_e(j, value):
        for wave in range(waves):
            eout_ref[wave, j] = value[wave * ROWS:(wave + 1) * ROWS] * 0.5

    def put_x(j, value):
        xs_ref[j] = value

    def put_y(j, value):
        ys_ref[j, 8:8 + both, :] = value
        for wave in range(waves):
            yend_ref[wave, j] = value[(wave + 1) * ROWS - 8:(wave + 1) * ROWS]

    def put_mat(j, value):
        mout_ref[j] = value

    loads[0].wait()
    spread_columns(block(e_ref), both, flip_ref, cols, put_e)
    stores[0].start()
    loads[1].wait()
    spread_columns(block(x_ref), both, flip2_ref, cols, put_x)
    loads[2].wait()
    spread_columns(block(y_ref), both, flip_ref, cols, put_y)
    lane = lax.broadcasted_iota(jnp.int32, (both, LANES), 1)
    row = lax.broadcasted_iota(jnp.int32, (both, LANES), 0)
    for j in range(cols):
        if j:
            xprev = xs_ref[j - 1]
        else:
            xprev = jnp.where(lane == 0, 0.0, pltpu.roll(xs_ref[cols - 1], 1, 1))
        yprev = jnp.where((row & (ROWS - 1)) == 0, 0.0, ys_ref[j, 7:7 + both, :])
        value = (ys_ref[j, 8:8 + both, :] - yprev) - (xs_ref[j] - xprev)
        for wave in range(waves):
            rout_ref[wave, j] = value[wave * ROWS:(wave + 1) * ROWS]
    stores[1].start()
    loads[3].wait()
    spread_columns(
        lambda j: mat_ref[:, j * LANES:(j + 1) * LANES].astype(jnp.float32), ROWS, flip2_ref, cols, put_mat)
    stores[2].start()
    for copy in stores:
        copy.wait()


def wrap_strips(ref, edge_ref, cols):
    rows = pl.ds(8, EXT - 16)
    lane = lax.broadcasted_iota(jnp.int32, (EXT - 16, LANES), 1)
    head, tail = ref[0, rows, :], ref[cols - 1, rows, :]
    edge_ref[1, rows, :] = jnp.where(lane == LANES - 1, 0.0, pltpu.roll(head, LANES - 1, 1))
    edge_ref[0, rows, :] = jnp.where(lane == 0, head, pltpu.roll(tail, 1, 1))


def wrap_strips(ref, edge_ref, cols):
    rows = pl.ds(8, EXT - 16)
    lane = lax.broadcasted_iota(jnp.int32, (EXT - 16, LANES), 1)
    head, tail = ref[0, rows, :], ref[cols - 1, rows, :]
    edge_ref[1, rows, :] = jnp.where(lane == LANES - 1, 0.0, pltpu.roll(head, LANES - 1, 1))
    edge_ref[0, rows, :] = jnp.where(lane == 0, head, pltpu.roll(tail, 1, 1))


def neighbours(ref, edge_ref, rows, base, cols):
    mid = [ref[j, rows, :] for j in range(cols)]
    across = [edge_ref[0, rows, :]] + mid + [edge_ref[1, rows, :]]

    def laplacian(j):
        down = ref[j, pl.ds(base + 1, 8), :] + ref[j, pl.ds(base - 1, 8), :]
        return (down + (across[j] + across[j + 2])) - 4.0 * mid[j]

    return mid, laplacian


def forward_kernel(
    waves, tiles, cols,
    coef_ref, table_ref, own_hbm, yend_ref, left_ref, right_ref, hot_ref,
    rot_hbm, spec_ref, q_hbm,
    rot_ref, q_ref, e_ref, eb_ref, rs_ref, mat_ref, line_ref, stage_ref, flip_ref, halo_ref, edge_ref, sems, out_sems,
):
    tile = lax.axis_index("tile")
    first, last = tile == 0, tile == tiles - 1
    copies = [pltpu.make_async_copy(own_hbm.at[2 * waves], mat_ref, sems.at[2 * waves])]
    for wave in range(waves):
        copies.append(pltpu.make_async_copy(
            own_hbm.at[wave], e_ref.at[wave, :, pl.ds(BASE, ROWS), :], sems.at[2 * wave]))
        copies.append(pltpu.make_async_copy(
            own_hbm.at[waves + wave], rs_ref.at[wave, :, pl.ds(BASE, ROWS), :], sems.at[2 * wave + 1]))
    for copy in copies:
        copy.start()
    size = left_ref.shape[0]
    left_row = 64
    stage_ref[0:size, :] = right_ref[...]
    stage_ref[left_row:left_row + size, :] = left_ref[...]

    def put(j, value):
        halo_ref[j] = value

    spread_columns(lambda j: stage_ref[:, j * LANES:(j + 1) * LANES], stage_ref.shape[0], flip_ref, cols, put)
    line_ref[...] = jnp.zeros(line_ref.shape, jnp.float32)
    copies[0].wait()
    for wave in range(waves):
        copies[1 + 2 * wave].wait()
        copies[2 + 2 * wave].wait()
        forward_wave(
            wave, waves, cols, first, last, coef_ref, table_ref, yend_ref, hot_ref, rot_ref, rot_hbm,
            q_ref, q_hbm, out_sems, e_ref.at[wave], eb_ref, rs_ref.at[wave], mat_ref, line_ref.at[wave], halo_ref, edge_ref)
    both = line_ref[...].reshape(2 * waves * ROWS, LANES)
    spectrum = 2.0 * lax.dot_general(
        jnp.ones((8, LANES), jnp.float32), both, (((1,), (1,)), ((), ())),
        precision=HIGHEST, preferred_element_type=jnp.float32)
    for at in range(0, tiles, 8):
        spec_ref[at:at + 8, :] = spectrum
    for wave in range(waves):
        pltpu.make_async_copy(q_ref.at[wave], q_hbm.at[wave], out_sems.at[wave, STEPS]).wait()
        for index in range(STEPS):
            pltpu.make_async_copy(
                rot_ref.at[wave, index], rot_hbm.at[wave, index], out_sems.at[wave, index]).wait()


def forward_wave(
    wave, waves, cols, first, last, coef_ref, table_ref, yend_ref, hot_ref,
    rots_ref, rot_hbm, qs_ref, q_hbm, out_sems, ea_ref, eb_ref, r_ref, mat_ref, line_ref, halo_ref, edge_ref,
):
    rot_ref, q_ref = rots_ref.at[wave], qs_ref.at[wave]
    hi = BASE + ROWS
    left, right = 64 + 2 * HALO * wave, 2 * HALO * wave
    mat_row = 2 * HALO * waves
    rates = [0.25 / jnp.broadcast_to(table_ref[wave:wave + 1, kind:kind + 1], (8, LANES))
             for kind in range(table_ref.shape[1])]

    def rate_of(mat):
        reps = mat.shape[0] // 8
        tall = [jnp.concatenate([rate] * reps, 0) if reps > 1 else rate for rate in rates]
        value = tall[0]
        for kind in range(1, len(tall)):
            value = jnp.where(mat == float(kind), tall[kind], value)
        return value

    top = lax.broadcasted_iota(jnp.int32, (8, LANES), 0) == 0
    zero = jnp.zeros((8, LANES), jnp.float32)
    for j in range(cols):
        ea_ref[j, 8:24, :] = halo_ref[j, left - 4:left + HALO, :]
        ea_ref[j, hi:hi + 16, :] = halo_ref[j, right:right + 16, :]
        eb_ref[j, hi:hi + 8, :] = zero
        r_ref[j, 8:24, :] = halo_ref[j, left + 7:left + 23, :]
        r_ref[j, BASE:BASE + 8, :] = r_ref[j, BASE:BASE + 8, :] - jnp.where(top, halo_ref[j, left + 23:left + 24, :], 0.0)
        r_ref[j, hi:hi + 8, :] = halo_ref[j, right + 12:right + 20, :] - jnp.where(top, yend_ref[wave, j, 7:8, :], 0.0)
        r_ref[j, hi + 8:hi + 16, :] = halo_ref[j, right + 20:right + 28, :]
        q_ref[j, 8:24, :] = rate_of(halo_ref[j, 64 + mat_row - 4:64 + mat_row + HALO, :])
        q_ref[j, hi:hi + 16, :] = rate_of(halo_ref[j, mat_row:mat_row + 16, :])

    def prepare(group, carry):
        own = pl.ds(group_rows(group - OWN_LO), 8)
        rows = pl.ds(group_rows(group), 8)
        for j in range(cols):
            q_ref[j, rows, :] = rate_of(mat_ref[j, own, :])
        return carry

    lax.fori_loop(OWN_LO, OWN_HI, prepare, 0)
    pltpu.make_async_copy(q_ref, q_hbm.at[wave], out_sems.at[wave, STEPS]).start()

    def mirror(ref):
        wrap_strips(ref, edge_ref, cols)

        @pl.when(first)
        def _():
            for j in range(cols):
                ref[j, BASE - 1:BASE, :] = ref[j, BASE:BASE + 1, :]

    mirror(ea_ref)

    def step(index, old_ref, new_ref):
        low, high = bounds(index, first, last)

        def turn(own, group, inner):
            base = group_rows(group)
            rows = pl.ds(base, 8)
            own_rows = pl.ds(group_rows(group - OWN_LO), 8)
            mid, laplacian = neighbours(old_ref, edge_ref, rows, base, cols)
            totals = [None, None]
            for j in range(cols):
                rotation = r_ref[j, rows, :] + laplacian(j)
                r_ref[j, rows, :] = rotation
                if own:
                    rot_ref[index, j, own_rows, :] = rotation
                enew = mid[j] + q_ref[j, rows, :] * rotation
                new_ref[j, rows, :] = enew
                if own:
                    term = enew * hot_ref[wave, j:j + 1, :]
                    totals[j % 2] = term if totals[j % 2] is None else totals[j % 2] + term
            if own:
                total = totals[0] + totals[1]
                line_ref[0, own_rows, :] = line_ref[0, own_rows, :] + total * coef_ref[wave, 0, index]
                line_ref[1, own_rows, :] = line_ref[1, own_rows, :] + total * coef_ref[wave, 1, index]
            return inner

        lax.fori_loop(low, OWN_LO, functools.partial(turn, False), 0)
        lax.fori_loop(OWN_LO, OWN_HI, functools.partial(turn, True), 0, unroll=2)
        lax.fori_loop(OWN_HI, high, functools.partial(turn, False), 0)
        mirror(new_ref)
        pltpu.make_async_copy(rot_ref.at[index], rot_hbm.at[wave, index], out_sems.at[wave, index]).start()

    def two_steps(pair, carry):
        step(2 * pair, ea_ref, eb_ref)
        step(2 * pair + 1, eb_ref, ea_ref)
        return carry

    lax.fori_loop(0, STEPS // 2, two_steps, 0)

def dot(left, right):
    return jnp.dot(left, right, preferred_element_type=jnp.float32)


def table_dot(table_ref, combo, value):
    high, low = halves(value)
    return dot(table_ref[combo, 0], high) + (dot(table_ref[combo, 0], low) + dot(table_ref[combo, 1], high))


def dot_table(value, table_ref, combo):
    high, low = halves(value)
    total = None
    for part, turn in ((0, lambda v: v), (1, turned)):
        upper, lower = turn(high), turn(low)
        term = dot(upper, table_ref[combo, part, 0]) + (
            dot(lower, table_ref[combo, part, 0]) + dot(upper, table_ref[combo, part, 1]))
        total = term if total is None else total + term
    return total


def turned(stacked):
    half = stacked.shape[0] // 2
    return jnp.concatenate([-stacked[half:], stacked[:half]], 0)


def chirp_part(tiles, waves, tile, tgt_ref, spectra_ref, tabs, eff_ref, bar_ref):
    left_ref, right_ref, back_ref, last_ref, twist_ref, chirp_ref = tabs
    count = tiles * NFREE
    pixel = iota2((NFREE, tiles), 1) * NFREE + iota2((NFREE, tiles), 0)
    srow, slane = iota2((8, LANES), 0), iota2((8, LANES), 1)
    effs = jnp.zeros((8, LANES), jnp.float32)
    spots = iota2((tiles, LANES), 0)
    every = [(wave, plane) for wave in range(waves) for plane in range(GROUP_PLANES)]
    lines = []
    for wave in range(waves):
        at = wave * LANES
        lines.append((spectra_ref[:, at:at + NFREE], spectra_ref[:, at + NFREE:at + LANES]))
    values = []
    for combo, (wave, _) in enumerate(every):
        ch_r, ch_i = chirp_ref[combo, 0], chirp_ref[combo, 1]
        real, imag = lines[wave]
        values.append(jnp.concatenate([ch_r * real - ch_i * imag, ch_r * imag + ch_i * real], 0))
    values = [table_dot(left_ref, combo, value) for combo, value in enumerate(values)]
    for combo, value in enumerate(values):
        tw_r, tw_i = twist_ref[combo, 0], twist_ref[combo, 1]
        st_r, st_i = value[:NFREE], value[NFREE:]
        values[combo] = jnp.concatenate([tw_r * st_r - tw_i * st_i, tw_r * st_i + tw_i * st_r], 0)
    values = [dot_table(value, right_ref, combo) for combo, value in enumerate(values)]
    hits, powers = [], []
    for (wave, plane), value in zip(every, values):
        f_r, f_i = value[:NFREE], value[NFREE:]
        intensity = f_r * f_r + f_i * f_i
        on_target = (pixel == tgt_ref[wave:wave + 1, plane:plane + 1]).astype(jnp.float32)
        hits.append(on_target)
        powers.append((jnp.sum(intensity * on_target, 0, keepdims=True), jnp.sum(intensity, 0, keepdims=True)))
    powers = [tuple(jnp.sum(power, 1, keepdims=True) for power in pair) for pair in powers]
    for combo, (wave, plane) in enumerate(every):
        target_power, total_power = powers[combo]
        mean_power = total_power / count + SMALL
        efficiency = target_power / mean_power
        weight = hits[combo] / mean_power - target_power / (mean_power * mean_power * count)
        effs = jnp.where((srow == wave) & (slane == plane), efficiency, effs)
        double = 2.0 * weight
        values[combo] = values[combo] * jnp.concatenate([double, double], 0)
    values = [dot_table(value, back_ref, combo) for combo, value in enumerate(values)]
    for combo, value in enumerate(values):
        tw_r, tw_i = twist_ref[combo, 0], twist_ref[combo, 1]
        st_r, st_i = value[:NFREE], value[NFREE:]
        values[combo] = jnp.concatenate([tw_r * st_r + tw_i * st_i, tw_r * st_i - tw_i * st_r], 0)
    values = [table_dot(last_ref, combo, value) for combo, value in enumerate(values)]
    for wave in range(waves):
        bar_real = jnp.zeros((tiles, NFREE), jnp.float32)
        bar_imag = jnp.zeros((tiles, NFREE), jnp.float32)
        for plane in range(GROUP_PLANES):
            combo = wave * GROUP_PLANES + plane
            ch_r, ch_i = chirp_ref[combo, 0], chirp_ref[combo, 1]
            l_r, l_i = values[combo][:tiles], values[combo][tiles:]
            bar_real = bar_real + ch_r * l_r + ch_i * l_i
            bar_imag = bar_imag + ch_r * l_i - ch_i * l_r
        for part, value in enumerate((bar_real, bar_imag)):
            for where, lo, hi, at in ((-1, NFREE - 16, NFREE, BASE - 16), (0, 0, NFREE, BASE), (1, 0, 16, BASE + ROWS)):
                chosen = (spots == tile + where).astype(jnp.float32)
                spread = lax.dot_general(
                    value, chosen, (((0,), (0,)), ((), ())), precision=HIGHEST, preferred_element_type=jnp.float32)
                bar_ref[wave, part, at:at + hi - lo, :] = spread[lo:hi]
    eff_ref[...] = effs


def adjoint_kernel(
    waves, tiles, cols,
    coef_ref, tgt_ref, spectra_ref, left_ref, right_ref, back_ref, last_ref, twist_ref, chirp_ref,
    hot_ref, rot_hbm, q_hbm,
    kept_ref, given_ref, eff_ref,
    bar_ref, e_ref, a_ref, sa_ref, sb_ref, prod_ref, flip_ref, edge_ref, grad_ref,
    rot_ref, q_ref, in_sems,
):
    tile = lax.axis_index("tile")
    first, last = tile == 0, tile == tiles - 1
    copies = [
        [pltpu.make_async_copy(q_hbm.at[wave], q_ref.at[wave], in_sems.at[wave, 0]),
         pltpu.make_async_copy(rot_hbm.at[wave], rot_ref.at[wave], in_sems.at[wave, 1])]
        for wave in range(waves)]
    for copy in copies[0] + copies[1]:
        copy.start()
    chirp_part(
        tiles, waves, tile, tgt_ref, spectra_ref,
        (left_ref, right_ref, back_ref, last_ref, twist_ref, chirp_ref), eff_ref, bar_ref)
    zero = jnp.zeros((8, LANES), jnp.float32)
    hi = BASE + ROWS
    for j in range(cols):
        sa_ref[j, hi:hi + 8, :] = zero
        sb_ref[j, hi:hi + 8, :] = zero

    def mirror(ref):
        wrap_strips(ref, edge_ref, cols)

        @pl.when(first)
        def _():
            for j in range(cols):
                ref[j, BASE - 1:BASE, :] = ref[j, BASE:BASE + 1, :]

    for wave in range(waves):
        for copy in copies[wave]:
            copy.wait()

        def pushed(rows, index):
            return (bar_ref[wave, 0, rows, :] * coef_ref[wave, 0, index]
                    + bar_ref[wave, 1, rows, :] * coef_ref[wave, 1, index])

        def step(count, old_ref, new_ref):
            index = STEPS - 1 - count
            low, high = bounds(count, first, last)

            def turn(own, group, inner):
                base = group_rows(group)
                rows = pl.ds(base, 8)
                own_rows = pl.ds(group_rows(group - OWN_LO), 8)
                push = pushed(rows, index)
                if old_ref is not None:
                    _, laplacian = neighbours(old_ref, edge_ref, rows, base, cols)
                for j in range(cols):
                    value = push * hot_ref[wave, j:j + 1, :]
                    if old_ref is None:
                        a_ref[j, rows, :] = zero
                    else:
                        slope = a_ref[j, rows, :] + laplacian(j)
                        a_ref[j, rows, :] = slope
                        value = (e_ref[j, rows, :] + slope) + value
                    e_ref[j, rows, :] = value
                    new_ref[j, rows, :] = q_ref[wave, j, rows, :] * value
                    if own:
                        product = value * rot_ref[wave, index, j, own_rows, :]
                        if old_ref is not None:
                            product = prod_ref[j, own_rows, :] + product
                        prod_ref[j, own_rows, :] = product
                return inner

            lax.fori_loop(low, OWN_LO, functools.partial(turn, False), 0)
            lax.fori_loop(OWN_LO, OWN_HI, functools.partial(turn, True), 0, unroll=2)
            lax.fori_loop(OWN_HI, high, functools.partial(turn, False), 0)
            mirror(new_ref)

        step(0, None, sa_ref)

        def two_steps(pair, carry):
            step(2 * pair + 1, sa_ref, sb_ref)
            step(2 * pair + 2, sb_ref, sa_ref)
            return carry

        lax.fori_loop(0, (STEPS - 2) // 2, two_steps, 0)

        def finish(group, carry):
            base = group_rows(group)
            rows = pl.ds(base, 8)
            own_rows = pl.ds(group_rows(group - OWN_LO), 8)
            push = pushed(rows, 0)
            _, laplacian = neighbours(sa_ref, edge_ref, rows, base, cols)
            for j in range(cols):
                value = (e_ref[j, rows, :] + (a_ref[j, rows, :] + laplacian(j))) + push * hot_ref[wave, j:j + 1, :]
                total = prod_ref[j, own_rows, :] + value * rot_ref[wave, 0, j, own_rows, :]
                rate = q_ref[wave, j, rows, :]
                total = total * (-8.0 * (rate * rate))
                if wave:
                    total = total + grad_ref[j, own_rows, :]
                grad_ref[j, own_rows, :] = total
            return carry

        lax.fori_loop(OWN_LO, OWN_HI, finish, 0)
    for j in range(cols):
        flip_ref[pl.ds(j, LANES, stride=cols), :ROWS] = grad_ref[j].T
    chips, wide = kept_ref.shape[0], kept_ref.shape[2] // LANES
    mine = lax.axis_index("wave")
    core, chip = lax.rem(mine, 2), lax.div(mine, 2)

    def emit(own_core):
        for j in range(cols):
            part = j // wide
            out = kept_ref if part % 2 == own_core else given_ref
            slot = lax.rem(part // 2 - chip + chips, chips)
            at = j % wide * LANES
            out[slot, :, at:at + LANES] = flip_ref[j * LANES:(j + 1) * LANES, :ROWS].T

    for own_core in range(2):
        pl.when(core == own_core)(functools.partial(emit, own_core))


def per_device(electric, magnet_x, magnet_y, permittivity_table, material, monitor_rows, targets):
    waves, rows, depth = electric.shape
    tiles = lax.axis_size("tile")
    parts = lax.axis_size("wave")
    cols = depth // LANES
    f32 = jnp.float32
    chips = parts // 2
    wave_ids = lax.axis_index("wave") * waves + jnp.arange(waves, dtype=jnp.int32)
    full = pltpu.CompilerParams(vmem_limit_bytes=VMEM_FULL * 1024 * 1024)
    lean = pltpu.CompilerParams(vmem_limit_bytes=VMEM_LEAN * 1024 * 1024)

    up = [(s, s + 1) for s in range(tiles - 1)]
    down = [(s + 1, s) for s in range(tiles - 1)]

    size = (2 * waves + 1) * HALO
    edges = pl.pallas_call(
        functools.partial(edges_kernel, waves),
        out_shape=(jax.ShapeDtypeStruct((size, depth), f32),) * 2,
        in_specs=[HSPEC] * 4,
        out_specs=(VSPEC,) * 2,
        scratch_shapes=[
            VMEM((2, waves, 3, 16, depth), f32), VMEM((2, 16, depth), jnp.int32),
            pltpu.SemaphoreType.DMA((2, waves, 4)),
        ],
        compiler_params=full,
        name="edges",
    )(electric, magnet_x, magnet_y, material)
    from_left = lax.ppermute(edges[0], "tile", up)
    from_right = lax.ppermute(edges[1], "tile", down)

    strip = (cols, rows, LANES)
    prepared = pl.pallas_call(
        functools.partial(prepare_kernel, waves, cols),
        out_shape=(
            jax.ShapeDtypeStruct((2 * waves + 1,) + strip, f32),
            jax.ShapeDtypeStruct((waves, cols, 8, LANES), f32),
        ),
        in_specs=[HSPEC] * 4,
        out_specs=(ASPEC, VSPEC),
        scratch_shapes=[
            VMEM((depth, LANES), f32), VMEM((depth, LANES), f32),
            VMEM((cols, waves * rows, LANES), f32), VMEM((cols, waves * rows + 8, LANES), f32),
            VMEM((waves, rows, depth), f32), VMEM((waves, rows, depth), f32), VMEM((waves, rows, depth), f32),
            VMEM((rows, depth), jnp.int32),
            VMEM((waves,) + strip, f32), VMEM((waves,) + strip, f32), VMEM(strip, f32),
            pltpu.SemaphoreType.DMA((7,)),
        ],
        compiler_params=lean,
        name="prepare",
    )(electric, magnet_x, magnet_y, material)

    combos = waves * GROUP_PLANES
    tables = pl.pallas_call(
        functools.partial(table_kernel, tiles, waves, 1.0 / math.sqrt(rows * tiles)),
        out_shape=(
            jax.ShapeDtypeStruct((combos, 2, 2 * NFREE, 2 * tiles), jnp.bfloat16),
            jax.ShapeDtypeStruct((combos, 2, 2, NFREE, tiles), jnp.bfloat16),
            jax.ShapeDtypeStruct((combos, 2, 2, tiles, NFREE), jnp.bfloat16),
            jax.ShapeDtypeStruct((combos, 2, 2 * tiles, 2 * NFREE), jnp.bfloat16),
            jax.ShapeDtypeStruct((combos, 2, NFREE, NFREE), f32),
            jax.ShapeDtypeStruct((combos, 2, tiles, NFREE), f32),
        ),
        in_specs=[],
        out_specs=(VSPEC,) * 6,
        compiler_params=full,
        name="tables",
    )()

    block = depth // monitor_rows.shape[1]
    row_ids = jnp.arange(cols, dtype=jnp.int32)[:, None] + cols * jnp.arange(LANES, dtype=jnp.int32)[None, :]
    lines = jnp.swapaxes(monitor_rows.reshape(waves, LANES, cols // block), 1, 2)
    hot = (jnp.repeat(lines, block, axis=1) == row_ids[None]).astype(f32)
    angular = 0.3 + 0.05 * wave_ids.astype(f32)
    phase = angular[:, None] * jnp.arange(1, STEPS + 1, dtype=jnp.int32).astype(f32)[None, :]
    coef = jnp.stack([jnp.cos(phase), -jnp.sin(phase)], 1)
    prepared, tables, hot, coef = lax.optimization_barrier((prepared, tables, hot, coef))
    own, y_end = prepared

    ext = (cols, EXT, LANES)
    rotations, spec, qs = pl.pallas_call(
        functools.partial(forward_kernel, waves, tiles, cols),
        out_shape=(
            jax.ShapeDtypeStruct((waves, STEPS) + strip, f32),
            jax.ShapeDtypeStruct((tiles, waves * LANES), f32),
            jax.ShapeDtypeStruct((waves,) + ext, f32),
        ),
        in_specs=[SSPEC, VSPEC, ASPEC] + [VSPEC] * 4,
        out_specs=(HSPEC, VSPEC, HSPEC),
        scratch_shapes=[
            VMEM((waves, STEPS) + strip, f32), VMEM((waves,) + ext, f32),
            VMEM((waves,) + ext, f32), VMEM(ext, f32), VMEM((waves,) + ext, f32),
            VMEM(strip, f32), VMEM((waves, 2, rows, LANES), f32),
            VMEM((LANES, depth), f32), VMEM((depth, LANES), f32), VMEM((cols, LANES, LANES), f32),
            VMEM((2, EXT, LANES), f32),
            pltpu.SemaphoreType.DMA((2 * waves + 1,)), pltpu.SemaphoreType.DMA((waves, STEPS + 1)),
        ],
        compiler_params=lean,
        name="forward",
    )(coef, permittivity_table, own, y_end, from_left, from_right, hot)

    gathered = lax.all_to_all(spec, "tile", 0, 0, tiled=True)

    kept, given, eff = pl.pallas_call(
        functools.partial(adjoint_kernel, waves, tiles, cols),
        out_shape=(
            jax.ShapeDtypeStruct((chips, rows, depth // parts), f32),
            jax.ShapeDtypeStruct((chips, rows, depth // parts), f32),
            jax.ShapeDtypeStruct((8, LANES), f32),
        ),
        in_specs=[SSPEC, VSPEC, VSPEC] + [VSPEC] * 6 + [VSPEC, HSPEC, HSPEC],
        out_specs=(VSPEC, VSPEC, VSPEC),
        scratch_shapes=[
            VMEM((waves, 2, EXT, LANES), f32),
            VMEM(ext, f32), VMEM(ext, f32), VMEM(ext, f32), VMEM(ext, f32),
            VMEM(strip, f32), VMEM((depth, LANES), f32),
            VMEM((2, EXT, LANES), f32), VMEM(strip, f32),
            VMEM((waves, STEPS) + strip, f32), VMEM((waves,) + ext, f32),
            pltpu.SemaphoreType.DMA((waves, 2)),
        ],
        compiler_params=full,
        name="adjoint",
    )(coef, targets, gathered, *tables, hot, rotations, qs)
    efficiency = eff[:waves, :GROUP_PLANES]

    swapped = lax.ppermute(given, "wave", [(s, s ^ 1) for s in range(parts)])
    half = [kept[hop] + swapped[hop] for hop in range(chips)]
    gradient = half[0]
    for hop in range(1, chips):
        gradient = gradient + lax.ppermute(
            half[hop], "wave", [(s, (s // 2 + hop) % chips * 2 + s % 2) for s in range(parts)])
    return gradient, efficiency


def solution(mesh):
    in_specs = (
        P("wave", "tile", None),
        P("wave", "tile", None),
        P("wave", "tile", None),
        P("wave", None),
        P("tile", None),
        P("wave", None),
        P("wave", None),
    )
    out_specs = (P("tile", "wave"), P("wave", None))
    return jax.shard_map(
        per_device, mesh=mesh, in_specs=in_specs, out_specs=out_specs, check_vma=False
    )
```

```python
import functools
import math

import jax
import jax.numpy as jnp
from jax import lax
from jax.experimental import pallas as pl
from jax.experimental.pallas import tpu as pltpu
from jax.sharding import PartitionSpec as P

STEPS = 12
GROUP_PLANES = 4
GROUPS = 2
PERIOD = 8192
SMALL = 1e-06

LANES = 128
ROWS = 64
HALO = 12
BASE = 24
EXT = 112
OWN_LO = BASE // 8
OWN_HI = (BASE + ROWS) // 8
NFREE = 64

VMEM_LEAN = 40
VMEM_FULL = 56
VMEM_TIGHT = 62_000_000
VMEM = pltpu.VMEM
VSPEC = pl.BlockSpec(memory_space=pltpu.VMEM)
SSPEC = pl.BlockSpec(memory_space=pltpu.SMEM)
ASPEC = pl.BlockSpec(memory_space=pl.ANY)
HSPEC = pl.BlockSpec(memory_space=pltpu.HBM)
HIGHEST = lax.Precision.HIGHEST


def cos_sin(phase):
    phase = phase & (PERIOD - 1)
    quadrant = (phase + 1024) >> 11
    angle = (phase - (quadrant << 11)).astype(jnp.float32) * (2.0 * math.pi / PERIOD)
    sq = angle * angle
    even = 1.0 + sq * (-1 / 2 + sq * (1 / 24 + sq * (-1 / 720 + sq * (1 / 40320))))
    odd = angle * (1.0 + sq * (-1 / 6 + sq * (1 / 120 + sq * (-1 / 5040 + sq * (1 / 362880)))))
    swap = (quadrant & 1) == 1
    cosine = jnp.where(swap, odd, even)
    sine = jnp.where(swap, even, odd)
    cosine = jnp.where(((quadrant + 1) & 2) != 0, -cosine, cosine)
    return cosine, jnp.where((quadrant & 2) != 0, -sine, sine)


def halves(value):
    high = value.astype(jnp.bfloat16)
    return high, (value - high.astype(jnp.float32)).astype(jnp.bfloat16)


def iota2(shape, axis):
    return lax.broadcasted_iota(jnp.int32, shape, axis)


def table_kernel(tiles, waves, scale, left_ref, right_ref, back_ref, last_ref, twist_ref, chirp_ref):
    unit = PERIOD // NFREE
    mine = lax.axis_index("wave")

    def one(combo, carry):
        wave = mine * waves + lax.div(combo, GROUP_PLANES)
        plane = GROUP_PLANES * lax.rem(wave, GROUPS) + lax.rem(combo, GROUP_PLANES)
        rate = 1 + lax.rem(37 * plane + 101 * wave, 509)

        def put(ref, slot, value):
            for which, part in enumerate(halves(value)):
                if slot is None:
                    ref[combo, which] = part
                else:
                    ref[combo, slot, which] = part

        shape = (NFREE, tiles)
        cosine, sine = cos_sin((iota2(shape, 0) * iota2(shape, 1) * rate & (NFREE - 1)) * unit)
        put(right_ref, 0, cosine)
        put(right_ref, 1, -sine)
        put(left_ref, None, jnp.concatenate(
            [jnp.concatenate([cosine, sine], 1), jnp.concatenate([-sine, cosine], 1)], 0))
        shape = (tiles, NFREE)
        cosine, sine = cos_sin((iota2(shape, 0) * iota2(shape, 1) * rate & (NFREE - 1)) * unit)
        put(back_ref, 0, cosine)
        put(back_ref, 1, sine)
        put(last_ref, None, jnp.concatenate(
            [jnp.concatenate([cosine, -sine], 1), jnp.concatenate([sine, cosine], 1)], 0))
        shape = (NFREE, NFREE)
        cosine, sine = cos_sin((iota2(shape, 0) * iota2(shape, 1) * rate & (PERIOD // 2 - 1)) * 2)
        twist_ref[combo, 0] = cosine
        twist_ref[combo, 1] = -sine
        shape = (tiles, NFREE)
        cell = iota2(shape, 0) * NFREE + iota2(shape, 1)
        cosine, sine = cos_sin((cell * cell & (PERIOD - 1)) * rate)
        chirp_ref[combo, 0] = cosine * scale
        chirp_ref[combo, 1] = sine * scale
        return carry

    lax.fori_loop(0, waves * GROUP_PLANES, one, 0)


def group_rows(group):
    return pl.multiple_of(group * 8, 8)


def bounds(step, first, last):
    low = jnp.where(step < 3, 1, jnp.where(step < STEPS - 1, 2, OWN_LO))
    high = jnp.where(step < 3, OWN_HI + 2, jnp.where(step < STEPS - 1, OWN_HI + 1, OWN_HI))
    return jnp.where(first, OWN_LO, low), jnp.where(last, OWN_HI, high)


def spread_columns(block_of, rows, flip_ref, cols, put):
    for j in range(cols):
        flip_ref[j * LANES:(j + 1) * LANES, :rows] = block_of(j).T
    for j in range(cols):
        put(j, flip_ref[pl.ds(j, LANES, stride=cols), :rows].T)


def edges_kernel(waves, e_hbm, x_hbm, y_hbm, mat_hbm, *refs):
    outs, (in_ref, mat_ref, sems) = refs[:2], refs[2:]
    span = 16
    copies = []
    for side, start in enumerate((ROWS - span, 0)):
        copies.append([pltpu.make_async_copy(mat_hbm.at[pl.ds(start, span), :], mat_ref.at[side], sems.at[side, 0, 3])])
        for wave in range(waves):
            copies.append([
                pltpu.make_async_copy(
                    src.at[wave, pl.ds(start, span), :], in_ref.at[side, wave, field], sems.at[side, wave, field])
                for field, src in enumerate((e_hbm, x_hbm, y_hbm))])
    for group in copies:
        for copy in group:
            copy.start()
    shape = in_ref.shape[3:]
    row, col = iota2(shape, 0), iota2(shape, 1)
    for side in range(2):
        for copy in copies[side * (waves + 1)]:
            copy.wait()
        for wave in range(waves):
            for copy in copies[side * (waves + 1) + 1 + wave]:
                copy.wait()
            out = outs[side].at[pl.ds(2 * HALO * wave, 2 * HALO), :]
            efield, xfield, yfield = in_ref[side, wave, 0], in_ref[side, wave, 1], in_ref[side, wave, 2]
            yprev = jnp.where(row == 0, 0.0, pltpu.roll(yfield, 1, 0))
            xprev = jnp.where(col == 0, 0.0, pltpu.roll(xfield, 1, 1))
            curl = (yfield - yprev) - (xfield - xprev)
            low = span - HALO
            if side:
                out[0:HALO, :] = efield[:HALO] * 0.5
                out[HALO:2 * HALO, :] = curl[:HALO]
            else:
                out[0:HALO, :] = efield[low:] * 0.5
                out[HALO:2 * HALO - 1, :] = curl[low + 1:]
                out[2 * HALO - 1:2 * HALO, :] = yfield[span - 1:]
        mat = mat_ref[side].astype(jnp.float32)
        outs[side][2 * HALO * waves:, :] = mat[:HALO] if side else mat[low:]


def prepare_kernel(
    waves, cols, e_hbm, x_hbm, y_hbm, mat_hbm, out_hbm, yend_ref,
    flip_ref, flip2_ref, xs_ref, ys_ref, e_ref, x_ref, y_ref, mat_ref, eout_ref, rout_ref, mout_ref, sems,
):
    both = waves * ROWS
    loads = [
        pltpu.make_async_copy(src, dst, sems.at[at])
        for at, (src, dst) in enumerate(((e_hbm, e_ref), (x_hbm, x_ref), (y_hbm, y_ref), (mat_hbm, mat_ref)))]
    stores = [
        pltpu.make_async_copy(src, dst, sems.at[4 + at])
        for at, (src, dst) in enumerate((
            (eout_ref, out_hbm.at[pl.ds(0, waves)]), (rout_ref, out_hbm.at[pl.ds(waves, waves)]),
            (mout_ref, out_hbm.at[2 * waves])))]
    for copy in loads:
        copy.start()

    def block(ref):
        return lambda j: ref[:, :, j * LANES:(j + 1) * LANES].reshape(both, LANES)

    def put_e(j, value):
        for wave in range(waves):
            eout_ref[wave, j] = value[wave * ROWS:(wave + 1) * ROWS] * 0.5

    def put_x(j, value):
        xs_ref[j] = value

    def put_y(j, value):
        ys_ref[j, 8:8 + both, :] = value
        for wave in range(waves):
            yend_ref[wave, j] = value[(wave + 1) * ROWS - 8:(wave + 1) * ROWS]

    def put_mat(j, value):
        mout_ref[j] = value

    loads[0].wait()
    spread_columns(block(e_ref), both, flip_ref, cols, put_e)
    stores[0].start()
    loads[1].wait()
    spread_columns(block(x_ref), both, flip2_ref, cols, put_x)
    loads[2].wait()
    spread_columns(block(y_ref), both, flip_ref, cols, put_y)
    lane = lax.broadcasted_iota(jnp.int32, (both, LANES), 1)
    row = lax.broadcasted_iota(jnp.int32, (both, LANES), 0)
    for j in range(cols):
        if j:
            xprev = xs_ref[j - 1]
        else:
            xprev = jnp.where(lane == 0, 0.0, pltpu.roll(xs_ref[cols - 1], 1, 1))
        yprev = jnp.where((row & (ROWS - 1)) == 0, 0.0, ys_ref[j, 7:7 + both, :])
        value = (ys_ref[j, 8:8 + both, :] - yprev) - (xs_ref[j] - xprev)
        for wave in range(waves):
            rout_ref[wave, j] = value[wave * ROWS:(wave + 1) * ROWS]
    stores[1].start()
    loads[3].wait()
    spread_columns(
        lambda j: mat_ref[:, j * LANES:(j + 1) * LANES].astype(jnp.float32), ROWS, flip2_ref, cols, put_mat)
    stores[2].start()
    for copy in stores:
        copy.wait()


def wrap_strips(ref, edge_ref, cols):
    rows = pl.ds(8, EXT - 16)
    lane = lax.broadcasted_iota(jnp.int32, (EXT - 16, LANES), 1)
    head, tail = ref[0, rows, :], ref[cols - 1, rows, :]
    edge_ref[1, rows, :] = jnp.where(lane == LANES - 1, 0.0, pltpu.roll(head, LANES - 1, 1))
    edge_ref[0, rows, :] = jnp.where(lane == 0, head, pltpu.roll(tail, 1, 1))


def wrap_strips(ref, edge_ref, cols):
    rows = pl.ds(8, EXT - 16)
    lane = lax.broadcasted_iota(jnp.int32, (EXT - 16, LANES), 1)
    head, tail = ref[0, rows, :], ref[cols - 1, rows, :]
    edge_ref[1, rows, :] = jnp.where(lane == LANES - 1, 0.0, pltpu.roll(head, LANES - 1, 1))
    edge_ref[0, rows, :] = jnp.where(lane == 0, head, pltpu.roll(tail, 1, 1))


def neighbours(ref, edge_ref, rows, base, cols):
    mid = [ref[j, rows, :] for j in range(cols)]
    across = [edge_ref[0, rows, :]] + mid + [edge_ref[1, rows, :]]

    def laplacian(j):
        down = ref[j, pl.ds(base + 1, 8), :] + ref[j, pl.ds(base - 1, 8), :]
        return (down + (across[j] + across[j + 2])) - 4.0 * mid[j]

    return mid, laplacian


def forward_kernel(
    waves, tiles, cols,
    coef_ref, table_ref, own_hbm, yend_ref, left_ref, right_ref, hot_ref,
    rot_hbm, spec_ref, q_hbm,
    rot_ref, q_ref, e_ref, eb_ref, rs_ref, mat_ref, line_ref, stage_ref, flip_ref, halo_ref, edge_ref, sems, out_sems,
):
    tile = lax.axis_index("tile")
    first, last = tile == 0, tile == tiles - 1
    copies = [pltpu.make_async_copy(own_hbm.at[2 * waves], mat_ref, sems.at[2 * waves])]
    for wave in range(waves):
        copies.append(pltpu.make_async_copy(
            own_hbm.at[wave], e_ref.at[wave, :, pl.ds(BASE, ROWS), :], sems.at[2 * wave]))
        copies.append(pltpu.make_async_copy(
            own_hbm.at[waves + wave], rs_ref.at[wave, :, pl.ds(BASE, ROWS), :], sems.at[2 * wave + 1]))
    for copy in copies:
        copy.start()
    size = left_ref.shape[0]
    left_row = 64
    stage_ref[0:size, :] = right_ref[...]
    stage_ref[left_row:left_row + size, :] = left_ref[...]

    def put(j, value):
        halo_ref[j] = value

    spread_columns(lambda j: stage_ref[:, j * LANES:(j + 1) * LANES], stage_ref.shape[0], flip_ref, cols, put)
    line_ref[...] = jnp.zeros(line_ref.shape, jnp.float32)
    copies[0].wait()
    for wave in range(waves):
        copies[1 + 2 * wave].wait()
        copies[2 + 2 * wave].wait()
        forward_wave(
            wave, waves, cols, first, last, coef_ref, table_ref, yend_ref, hot_ref, rot_ref, rot_hbm,
            q_ref, q_hbm, out_sems, e_ref.at[wave], eb_ref, rs_ref.at[wave], mat_ref, line_ref.at[wave], halo_ref, edge_ref)
    both = line_ref[...].reshape(2 * waves * ROWS, LANES)
    spectrum = 2.0 * lax.dot_general(
        jnp.ones((8, LANES), jnp.float32), both, (((1,), (1,)), ((), ())),
        precision=HIGHEST, preferred_element_type=jnp.float32)
    for at in range(0, tiles, 8):
        spec_ref[at:at + 8, :] = spectrum
    for wave in range(waves):
        pltpu.make_async_copy(q_ref.at[wave], q_hbm.at[wave], out_sems.at[wave, STEPS]).wait()
        for index in range(STEPS):
            pltpu.make_async_copy(
                rot_ref.at[wave, index], rot_hbm.at[wave, index], out_sems.at[wave, index]).wait()


def forward_wave(
    wave, waves, cols, first, last, coef_ref, table_ref, yend_ref, hot_ref,
    rots_ref, rot_hbm, qs_ref, q_hbm, out_sems, ea_ref, eb_ref, r_ref, mat_ref, line_ref, halo_ref, edge_ref,
):
    rot_ref, q_ref = rots_ref.at[wave], qs_ref.at[wave]
    hi = BASE + ROWS
    left, right = 64 + 2 * HALO * wave, 2 * HALO * wave
    mat_row = 2 * HALO * waves
    rates = [0.25 / jnp.broadcast_to(table_ref[wave:wave + 1, kind:kind + 1], (8, LANES))
             for kind in range(table_ref.shape[1])]

    def rate_of(mat):
        reps = mat.shape[0] // 8
        tall = [jnp.concatenate([rate] * reps, 0) if reps > 1 else rate for rate in rates]
        value = tall[0]
        for kind in range(1, len(tall)):
            value = jnp.where(mat == float(kind), tall[kind], value)
        return value

    top = lax.broadcasted_iota(jnp.int32, (8, LANES), 0) == 0
    zero = jnp.zeros((8, LANES), jnp.float32)
    for j in range(cols):
        ea_ref[j, 8:24, :] = halo_ref[j, left - 4:left + HALO, :]
        ea_ref[j, hi:hi + 16, :] = halo_ref[j, right:right + 16, :]
        eb_ref[j, hi:hi + 8, :] = zero
        r_ref[j, 8:24, :] = halo_ref[j, left + 7:left + 23, :]
        r_ref[j, BASE:BASE + 8, :] = r_ref[j, BASE:BASE + 8, :] - jnp.where(top, halo_ref[j, left + 23:left + 24, :], 0.0)
        r_ref[j, hi:hi + 8, :] = halo_ref[j, right + 12:right + 20, :] - jnp.where(top, yend_ref[wave, j, 7:8, :], 0.0)
        r_ref[j, hi + 8:hi + 16, :] = halo_ref[j, right + 20:right + 28, :]
        q_ref[j, 8:24, :] = rate_of(halo_ref[j, 64 + mat_row - 4:64 + mat_row + HALO, :])
        q_ref[j, hi:hi + 16, :] = rate_of(halo_ref[j, mat_row:mat_row + 16, :])

    def prepare(group, carry):
        own = pl.ds(group_rows(group - OWN_LO), 8)
        rows = pl.ds(group_rows(group), 8)
        for j in range(cols):
            q_ref[j, rows, :] = rate_of(mat_ref[j, own, :])
        return carry

    lax.fori_loop(OWN_LO, OWN_HI, prepare, 0)
    pltpu.make_async_copy(q_ref, q_hbm.at[wave], out_sems.at[wave, STEPS]).start()

    def mirror(ref):
        wrap_strips(ref, edge_ref, cols)

        @pl.when(first)
        def _():
            for j in range(cols):
                ref[j, BASE - 1:BASE, :] = ref[j, BASE:BASE + 1, :]

    mirror(ea_ref)

    def step(index, old_ref, new_ref):
        low, high = bounds(index, first, last)

        def turn(own, group, inner):
            base = group_rows(group)
            rows = pl.ds(base, 8)
            own_rows = pl.ds(group_rows(group - OWN_LO), 8)
            mid, laplacian = neighbours(old_ref, edge_ref, rows, base, cols)
            totals = [None, None]
            for j in range(cols):
                rotation = r_ref[j, rows, :] + laplacian(j)
                r_ref[j, rows, :] = rotation
                if own:
                    rot_ref[index, j, own_rows, :] = rotation
                enew = mid[j] + q_ref[j, rows, :] * rotation
                new_ref[j, rows, :] = enew
                if own:
                    term = enew * hot_ref[wave, j:j + 1, :]
                    totals[j % 2] = term if totals[j % 2] is None else totals[j % 2] + term
            if own:
                total = totals[0] + totals[1]
                line_ref[0, own_rows, :] = line_ref[0, own_rows, :] + total * coef_ref[wave, 0, index]
                line_ref[1, own_rows, :] = line_ref[1, own_rows, :] + total * coef_ref[wave, 1, index]
            return inner

        lax.fori_loop(low, OWN_LO, functools.partial(turn, False), 0)
        lax.fori_loop(OWN_LO, OWN_HI, functools.partial(turn, True), 0, unroll=4)
        lax.fori_loop(OWN_HI, high, functools.partial(turn, False), 0)
        mirror(new_ref)
        pltpu.make_async_copy(rot_ref.at[index], rot_hbm.at[wave, index], out_sems.at[wave, index]).start()

    def two_steps(pair, carry):
        step(2 * pair, ea_ref, eb_ref)
        step(2 * pair + 1, eb_ref, ea_ref)
        return carry

    lax.fori_loop(0, STEPS // 2, two_steps, 0)

def dot(left, right):
    return jnp.dot(left, right, preferred_element_type=jnp.float32)


def table_dot(table_ref, combo, value):
    high, low = halves(value)
    return dot(table_ref[combo, 0], high) + (dot(table_ref[combo, 0], low) + dot(table_ref[combo, 1], high))


def dot_table(value, table_ref, combo):
    high, low = halves(value)
    total = None
    for part, turn in ((0, lambda v: v), (1, turned)):
        upper, lower = turn(high), turn(low)
        term = dot(upper, table_ref[combo, part, 0]) + (
            dot(lower, table_ref[combo, part, 0]) + dot(upper, table_ref[combo, part, 1]))
        total = term if total is None else total + term
    return total


def turned(stacked):
    half = stacked.shape[0] // 2
    return jnp.concatenate([-stacked[half:], stacked[:half]], 0)


def chirp_part(tiles, waves, tile, tgt_ref, spectra_ref, tabs, eff_ref, bar_ref):
    left_ref, right_ref, back_ref, last_ref, twist_ref, chirp_ref = tabs
    count = tiles * NFREE
    pixel = iota2((NFREE, tiles), 1) * NFREE + iota2((NFREE, tiles), 0)
    srow, slane = iota2((8, LANES), 0), iota2((8, LANES), 1)
    effs = jnp.zeros((8, LANES), jnp.float32)
    spots = iota2((tiles, LANES), 0)
    every = [(wave, plane) for wave in range(waves) for plane in range(GROUP_PLANES)]
    lines = []
    for wave in range(waves):
        at = wave * LANES
        lines.append((spectra_ref[:, at:at + NFREE], spectra_ref[:, at + NFREE:at + LANES]))
    values = []
    for combo, (wave, _) in enumerate(every):
        ch_r, ch_i = chirp_ref[combo, 0], chirp_ref[combo, 1]
        real, imag = lines[wave]
        values.append(jnp.concatenate([ch_r * real - ch_i * imag, ch_r * imag + ch_i * real], 0))
    values = [table_dot(left_ref, combo, value) for combo, value in enumerate(values)]
    for combo, value in enumerate(values):
        tw_r, tw_i = twist_ref[combo, 0], twist_ref[combo, 1]
        st_r, st_i = value[:NFREE], value[NFREE:]
        values[combo] = jnp.concatenate([tw_r * st_r - tw_i * st_i, tw_r * st_i + tw_i * st_r], 0)
    values = [dot_table(value, right_ref, combo) for combo, value in enumerate(values)]
    hits, powers = [], []
    for (wave, plane), value in zip(every, values):
        f_r, f_i = value[:NFREE], value[NFREE:]
        intensity = f_r * f_r + f_i * f_i
        on_target = (pixel == tgt_ref[wave:wave + 1, plane:plane + 1]).astype(jnp.float32)
        hits.append(on_target)
        powers.append((jnp.sum(intensity * on_target, 0, keepdims=True), jnp.sum(intensity, 0, keepdims=True)))
    powers = [tuple(jnp.sum(power, 1, keepdims=True) for power in pair) for pair in powers]
    for combo, (wave, plane) in enumerate(every):
        target_power, total_power = powers[combo]
        mean_power = total_power / count + SMALL
        efficiency = target_power / mean_power
        weight = hits[combo] / mean_power - target_power / (mean_power * mean_power * count)
        effs = jnp.where((srow == wave) & (slane == plane), efficiency, effs)
        double = 2.0 * weight
        values[combo] = values[combo] * jnp.concatenate([double, double], 0)
    values = [dot_table(value, back_ref, combo) for combo, value in enumerate(values)]
    for combo, value in enumerate(values):
        tw_r, tw_i = twist_ref[combo, 0], twist_ref[combo, 1]
        st_r, st_i = value[:NFREE], value[NFREE:]
        values[combo] = jnp.concatenate([tw_r * st_r + tw_i * st_i, tw_r * st_i - tw_i * st_r], 0)
    values = [table_dot(last_ref, combo, value) for combo, value in enumerate(values)]
    for wave in range(waves):
        bar_real = jnp.zeros((tiles, NFREE), jnp.float32)
        bar_imag = jnp.zeros((tiles, NFREE), jnp.float32)
        for plane in range(GROUP_PLANES):
            combo = wave * GROUP_PLANES + plane
            ch_r, ch_i = chirp_ref[combo, 0], chirp_ref[combo, 1]
            l_r, l_i = values[combo][:tiles], values[combo][tiles:]
            bar_real = bar_real + ch_r * l_r + ch_i * l_i
            bar_imag = bar_imag + ch_r * l_i - ch_i * l_r
        for part, value in enumerate((bar_real, bar_imag)):
            for where, lo, hi, at in ((-1, NFREE - 16, NFREE, BASE - 16), (0, 0, NFREE, BASE), (1, 0, 16, BASE + ROWS)):
                chosen = (spots == tile + where).astype(jnp.float32)
                spread = lax.dot_general(
                    value, chosen, (((0,), (0,)), ((), ())), precision=HIGHEST, preferred_element_type=jnp.float32)
                bar_ref[wave, part, at:at + hi - lo, :] = spread[lo:hi]
    eff_ref[...] = effs


def adjoint_kernel(
    waves, tiles, cols,
    coef_ref, tgt_ref, spectra_ref, left_ref, right_ref, back_ref, last_ref, twist_ref, chirp_ref,
    hot_ref, rot_hbm, q_hbm,
    kept_ref, given_ref, eff_ref,
    bar_ref, e_ref, a_ref, sa_ref, sb_ref, prod_ref, flip_ref, edge_ref, grad_ref,
    rot_ref, q_ref, in_sems,
):
    tile = lax.axis_index("tile")
    first, last = tile == 0, tile == tiles - 1
    copies = [
        [pltpu.make_async_copy(q_hbm.at[wave], q_ref.at[wave], in_sems.at[wave, 0]),
         pltpu.make_async_copy(rot_hbm.at[wave], rot_ref.at[wave], in_sems.at[wave, 1])]
        for wave in range(waves)]
    for copy in copies[0] + copies[1]:
        copy.start()
    chirp_part(
        tiles, waves, tile, tgt_ref, spectra_ref,
        (left_ref, right_ref, back_ref, last_ref, twist_ref, chirp_ref), eff_ref, bar_ref)
    zero = jnp.zeros((8, LANES), jnp.float32)
    hi = BASE + ROWS
    for j in range(cols):
        sa_ref[j, hi:hi + 8, :] = zero
        sb_ref[j, hi:hi + 8, :] = zero

    def mirror(ref):
        wrap_strips(ref, edge_ref, cols)

        @pl.when(first)
        def _():
            for j in range(cols):
                ref[j, BASE - 1:BASE, :] = ref[j, BASE:BASE + 1, :]

    for wave in range(waves):
        for copy in copies[wave]:
            copy.wait()

        def pushed(rows, index):
            return (bar_ref[wave, 0, rows, :] * coef_ref[wave, 0, index]
                    + bar_ref[wave, 1, rows, :] * coef_ref[wave, 1, index])

        def step(count, old_ref, new_ref):
            index = STEPS - 1 - count
            low, high = bounds(count, first, last)

            def turn(own, group, inner):
                base = group_rows(group)
                rows = pl.ds(base, 8)
                own_rows = pl.ds(group_rows(group - OWN_LO), 8)
                push = pushed(rows, index)
                if old_ref is not None:
                    _, laplacian = neighbours(old_ref, edge_ref, rows, base, cols)
                for j in range(cols):
                    value = push * hot_ref[wave, j:j + 1, :]
                    if old_ref is None:
                        a_ref[j, rows, :] = zero
                    else:
                        slope = a_ref[j, rows, :] + laplacian(j)
                        a_ref[j, rows, :] = slope
                        value = (e_ref[j, rows, :] + slope) + value
                    e_ref[j, rows, :] = value
                    new_ref[j, rows, :] = q_ref[wave, j, rows, :] * value
                    if own:
                        product = value * rot_ref[wave, index, j, own_rows, :]
                        if old_ref is not None:
                            product = prod_ref[j, own_rows, :] + product
                        prod_ref[j, own_rows, :] = product
                return inner

            lax.fori_loop(low, OWN_LO, functools.partial(turn, False), 0)
            lax.fori_loop(OWN_LO, OWN_HI, functools.partial(turn, True), 0, unroll=4)
            lax.fori_loop(OWN_HI, high, functools.partial(turn, False), 0)
            mirror(new_ref)

        step(0, None, sa_ref)

        def two_steps(pair, carry):
            step(2 * pair + 1, sa_ref, sb_ref)
            step(2 * pair + 2, sb_ref, sa_ref)
            return carry

        lax.fori_loop(0, (STEPS - 2) // 2, two_steps, 0)

        def finish(group, carry):
            base = group_rows(group)
            rows = pl.ds(base, 8)
            own_rows = pl.ds(group_rows(group - OWN_LO), 8)
            push = pushed(rows, 0)
            _, laplacian = neighbours(sa_ref, edge_ref, rows, base, cols)
            for j in range(cols):
                value = (e_ref[j, rows, :] + (a_ref[j, rows, :] + laplacian(j))) + push * hot_ref[wave, j:j + 1, :]
                total = prod_ref[j, own_rows, :] + value * rot_ref[wave, 0, j, own_rows, :]
                rate = q_ref[wave, j, rows, :]
                total = total * (-8.0 * (rate * rate))
                if wave:
                    total = total + grad_ref[j, own_rows, :]
                grad_ref[j, own_rows, :] = total
            return carry

        lax.fori_loop(OWN_LO, OWN_HI, finish, 0)
    for j in range(cols):
        flip_ref[pl.ds(j, LANES, stride=cols), :ROWS] = grad_ref[j].T
    chips, wide = kept_ref.shape[0], kept_ref.shape[2] // LANES
    mine = lax.axis_index("wave")
    core, chip = lax.rem(mine, 2), lax.div(mine, 2)

    def emit(own_core):
        for j in range(cols):
            part = j // wide
            out = kept_ref if part % 2 == own_core else given_ref
            slot = lax.rem(part // 2 - chip + chips, chips)
            at = j % wide * LANES
            out[slot, :, at:at + LANES] = flip_ref[j * LANES:(j + 1) * LANES, :ROWS].T

    for own_core in range(2):
        pl.when(core == own_core)(functools.partial(emit, own_core))


def per_device(electric, magnet_x, magnet_y, permittivity_table, material, monitor_rows, targets):
    waves, rows, depth = electric.shape
    tiles = lax.axis_size("tile")
    parts = lax.axis_size("wave")
    cols = depth // LANES
    f32 = jnp.float32
    chips = parts // 2
    wave_ids = lax.axis_index("wave") * waves + jnp.arange(waves, dtype=jnp.int32)
    full = pltpu.CompilerParams(vmem_limit_bytes=VMEM_FULL * 1024 * 1024)
    tight = pltpu.CompilerParams(vmem_limit_bytes=VMEM_TIGHT)
    lean = pltpu.CompilerParams(vmem_limit_bytes=VMEM_LEAN * 1024 * 1024)

    up = [(s, s + 1) for s in range(tiles - 1)]
    down = [(s + 1, s) for s in range(tiles - 1)]

    size = (2 * waves + 1) * HALO
    edges = pl.pallas_call(
        functools.partial(edges_kernel, waves),
        out_shape=(jax.ShapeDtypeStruct((size, depth), f32),) * 2,
        in_specs=[HSPEC] * 4,
        out_specs=(VSPEC,) * 2,
        scratch_shapes=[
            VMEM((2, waves, 3, 16, depth), f32), VMEM((2, 16, depth), jnp.int32),
            pltpu.SemaphoreType.DMA((2, waves, 4)),
        ],
        compiler_params=full,
        name="edges",
    )(electric, magnet_x, magnet_y, material)
    from_left = lax.ppermute(edges[0], "tile", up)
    from_right = lax.ppermute(edges[1], "tile", down)

    strip = (cols, rows, LANES)
    prepared = pl.pallas_call(
        functools.partial(prepare_kernel, waves, cols),
        out_shape=(
            jax.ShapeDtypeStruct((2 * waves + 1,) + strip, f32),
            jax.ShapeDtypeStruct((waves, cols, 8, LANES), f32),
        ),
        in_specs=[HSPEC] * 4,
        out_specs=(ASPEC, VSPEC),
        scratch_shapes=[
            VMEM((depth, LANES), f32), VMEM((depth, LANES), f32),
            VMEM((cols, waves * rows, LANES), f32), VMEM((cols, waves * rows + 8, LANES), f32),
            VMEM((waves, rows, depth), f32), VMEM((waves, rows, depth), f32), VMEM((waves, rows, depth), f32),
            VMEM((rows, depth), jnp.int32),
            VMEM((waves,) + strip, f32), VMEM((waves,) + strip, f32), VMEM(strip, f32),
            pltpu.SemaphoreType.DMA((7,)),
        ],
        compiler_params=lean,
        name="prepare",
    )(electric, magnet_x, magnet_y, material)

    combos = waves * GROUP_PLANES
    tables = pl.pallas_call(
        functools.partial(table_kernel, tiles, waves, 1.0 / math.sqrt(rows * tiles)),
        out_shape=(
            jax.ShapeDtypeStruct((combos, 2, 2 * NFREE, 2 * tiles), jnp.bfloat16),
            jax.ShapeDtypeStruct((combos, 2, 2, NFREE, tiles), jnp.bfloat16),
            jax.ShapeDtypeStruct((combos, 2, 2, tiles, NFREE), jnp.bfloat16),
            jax.ShapeDtypeStruct((combos, 2, 2 * tiles, 2 * NFREE), jnp.bfloat16),
            jax.ShapeDtypeStruct((combos, 2, NFREE, NFREE), f32),
            jax.ShapeDtypeStruct((combos, 2, tiles, NFREE), f32),
        ),
        in_specs=[],
        out_specs=(VSPEC,) * 6,
        compiler_params=full,
        name="tables",
    )()

    block = depth // monitor_rows.shape[1]
    row_ids = jnp.arange(cols, dtype=jnp.int32)[:, None] + cols * jnp.arange(LANES, dtype=jnp.int32)[None, :]
    lines = jnp.swapaxes(monitor_rows.reshape(waves, LANES, cols // block), 1, 2)
    hot = (jnp.repeat(lines, block, axis=1) == row_ids[None]).astype(f32)
    angular = 0.3 + 0.05 * wave_ids.astype(f32)
    phase = angular[:, None] * jnp.arange(1, STEPS + 1, dtype=jnp.int32).astype(f32)[None, :]
    coef = jnp.stack([jnp.cos(phase), -jnp.sin(phase)], 1)
    prepared, tables, hot, coef = lax.optimization_barrier((prepared, tables, hot, coef))
    own, y_end = prepared

    ext = (cols, EXT, LANES)
    rotations, spec, qs = pl.pallas_call(
        functools.partial(forward_kernel, waves, tiles, cols),
        out_shape=(
            jax.ShapeDtypeStruct((waves, STEPS) + strip, f32),
            jax.ShapeDtypeStruct((tiles, waves * LANES), f32),
            jax.ShapeDtypeStruct((waves,) + ext, f32),
        ),
        in_specs=[SSPEC, VSPEC, ASPEC] + [VSPEC] * 4,
        out_specs=(HSPEC, VSPEC, HSPEC),
        scratch_shapes=[
            VMEM((waves, STEPS) + strip, f32), VMEM((waves,) + ext, f32),
            VMEM((waves,) + ext, f32), VMEM(ext, f32), VMEM((waves,) + ext, f32),
            VMEM(strip, f32), VMEM((waves, 2, rows, LANES), f32),
            VMEM((LANES, depth), f32), VMEM((depth, LANES), f32), VMEM((cols, LANES, LANES), f32),
            VMEM((2, EXT, LANES), f32),
            pltpu.SemaphoreType.DMA((2 * waves + 1,)), pltpu.SemaphoreType.DMA((waves, STEPS + 1)),
        ],
        compiler_params=tight,
        name="forward",
    )(coef, permittivity_table, own, y_end, from_left, from_right, hot)

    gathered = lax.all_to_all(spec, "tile", 0, 0, tiled=True)

    kept, given, eff = pl.pallas_call(
        functools.partial(adjoint_kernel, waves, tiles, cols),
        out_shape=(
            jax.ShapeDtypeStruct((chips, rows, depth // parts), f32),
            jax.ShapeDtypeStruct((chips, rows, depth // parts), f32),
            jax.ShapeDtypeStruct((8, LANES), f32),
        ),
        in_specs=[SSPEC, VSPEC, VSPEC] + [VSPEC] * 6 + [VSPEC, HSPEC, HSPEC],
        out_specs=(VSPEC, VSPEC, VSPEC),
        scratch_shapes=[
            VMEM((waves, 2, EXT, LANES), f32),
            VMEM(ext, f32), VMEM(ext, f32), VMEM(ext, f32), VMEM(ext, f32),
            VMEM(strip, f32), VMEM((depth, LANES), f32),
            VMEM((2, EXT, LANES), f32), VMEM(strip, f32),
            VMEM((waves, STEPS) + strip, f32), VMEM((waves,) + ext, f32),
            pltpu.SemaphoreType.DMA((waves, 2)),
        ],
        compiler_params=full,
        name="adjoint",
    )(coef, targets, gathered, *tables, hot, rotations, qs)
    efficiency = eff[:waves, :GROUP_PLANES]

    swapped = lax.ppermute(given, "wave", [(s, s ^ 1) for s in range(parts)])
    half = [kept[hop] + swapped[hop] for hop in range(chips)]
    gradient = half[0]
    for hop in range(1, chips):
        gradient = gradient + lax.ppermute(
            half[hop], "wave", [(s, (s // 2 + hop) % chips * 2 + s % 2) for s in range(parts)])
    return gradient, efficiency


def solution(mesh):
    in_specs = (
        P("wave", "tile", None),
        P("wave", "tile", None),
        P("wave", "tile", None),
        P("wave", None),
        P("tile", None),
        P("wave", None),
        P("wave", None),
    )
    out_specs = (P("tile", "wave"), P("wave", None))
    return jax.shard_map(
        per_device, mesh=mesh, in_specs=in_specs, out_specs=out_specs, check_vma=False
    )
```
